256 devices in a mesh: row: 32 (over z, y), col: 8 (over x, core).
Axes of the slice: x: 4, y: 4, z: 8, core: 2. Of those that a mesh axis runs over, the one named last changes fastest.
Arguments:
- embeddings: bfloat16 [262144, 1024], P('row', 'col'), may hold values from -0.1875 to 0.1875
- quality: float32 [262144], P('row'), may hold values from 0.5 to 2
- probes: float32 [32, 262144], P(None, 'row'), may hold values from -6 to 6
- neighbors: int32 [2048, 8], P('row'), may hold values from 0 to 2047, as said below
Outputs:
- first: float32 [32, 262144], P(None, 'row')
- second: float32 [32, 262144], P(None, 'row')
The draws below stay inside these ranges and needn't reach their ends.
Inputs may be any that keep to these rules, and one draw needn't show every extreme that they name: `neighbors`: block b is held by row index b // 64. Among the 512 entries of one row index's blocks, at most 8 name blocks of any one other row index, and on every row index some other index is named exactly 8 times; the remaining entries name the index's own blocks.
All inputs are finite; a program needn't handle non-finite values.
Results may differ from the reference program's by a relative error of at most 0.02.
Values may be sent and summed in bfloat16 or wider, within the bound.
A program may use at most 64 MiB of HBM per device.

```python
import math
import jax
import jax.numpy as jnp
from jax import lax

EMB = 1024
BS = 128
PROBES = 32
KN = 8
BLK_DEV = 64
NBLK = 2048
NDOC = 262144
CAP = 8
N_ROW = 32
N_COL = 8


def draw_neighbors(key, part):
    entries = BLK_DEV * KN
    key_count, key_force, key_perm, key_local = jax.random.split(jax.random.fold_in(key, 17), 4)
    counts = jax.random.randint(key_count, (N_ROW, N_ROW), CAP // 4, CAP + 1)
    offsets = jnp.arange(N_ROW, dtype=jnp.int32)
    forced = jax.random.randint(key_force, (N_ROW,), 1, N_ROW)
    counts = jnp.where(offsets[None, :] == forced[:, None], CAP, counts)
    counts = jnp.where(offsets[None, :] == 0, 0, counts)
    bounds = jnp.cumsum(counts, axis=1)
    perm_keys = jax.random.split(key_perm, N_ROW)
    ranks = jax.vmap(lambda one_key: jax.random.permutation(one_key, entries))(perm_keys).astype(jnp.int32)
    offset = jnp.sum((ranks[:, :, None] >= bounds[:, None, :]).astype(jnp.int32), axis=2)
    offset = jnp.where(offset >= N_ROW, 0, offset)
    owner = (offsets[:, None] + offset) % N_ROW
    local = jax.random.randint(key_local, (N_ROW, entries), 0, BLK_DEV)
    return (owner * BLK_DEV + local).astype(jnp.int32).reshape(NBLK, KN)


def shard_levels(stream_key, extent, shards, least, top_value):
    def one(dim, parts):
        steps = jax.random.uniform(jax.random.fold_in(jax.random.fold_in(stream_key, 6), dim), (parts,), jnp.float32, least / len(shards), top_value / len(shards))
        return jnp.repeat(jnp.exp(steps), extent[dim] // parts).reshape((-1,) + (1,) * (len(extent) - dim - 1))

    gain = one(*shards[0])
    for cut in shards[1:]:
        gain = gain * one(*cut)
    return gain


def gaussian(stream_key, extent, spread, most, cuts=(), kind=jnp.bfloat16):
    gain = shard_levels(stream_key, extent, cuts, -0.22, 0.18) if cuts else 1.0
    drawn = jax.random.normal(stream_key, extent, jnp.float32) * spread * gain
    return jnp.minimum(jnp.maximum(drawn, -most), most).astype(kind)


def setup_inputs(seed: int = 0) -> dict:
    key_of = jax.random.split(jax.random.key(seed), 5)
    embeddings = gaussian(key_of[0], (NDOC, EMB), EMB ** -0.5, 0.1875, ((0, 32), (1, 8)))
    quality = jnp.clip(jnp.exp(math.log(2.0) - 1.3862944 * jax.random.uniform(key_of[1], (NDOC,), jnp.float32) ** shard_levels(key_of[1], (NDOC,), ((0, 32),), -0.2, 0.2)), 0.5, 2.0)
    probes = gaussian(key_of[2], (PROBES, NDOC), 1.0, 6.0, ((1, 32),), jnp.float32)
    neighbors = draw_neighbors(jax.random.fold_in(key_of[4], 71), 0)
    return dict(embeddings=embeddings, quality=quality, probes=probes, neighbors=neighbors)


def reference(embeddings, quality, probes, neighbors):
    width = EMB // N_COL
    blocks = embeddings.reshape(N_ROW, BLK_DEV, BS, N_COL, width)
    lists = neighbors.reshape(N_ROW, BLK_DEV, KN)

    def block_sums(vec):
        scaled = (vec * quality[None, :]).astype(jnp.bfloat16).reshape(PROBES, N_ROW, BLK_DEV, BS)
        scaled = jnp.moveaxis(scaled, 1, 0)

        def one_shard(pair):
            emb, weights = pair
            return jnp.einsum("bdsc,pbd->bscp", emb.astype(jnp.float32), weights.astype(jnp.float32)).astype(jnp.bfloat16)

        return lax.map(one_shard, (blocks, scaled)).reshape(NBLK, N_COL, width, PROBES)

    def apply(vec):
        sums = block_sums(vec)

        def one_shard(pair):
            emb, ids = pair
            gathered = jnp.sum(sums[ids].astype(jnp.float32), axis=1).astype(jnp.bfloat16)
            partial_value = jnp.einsum("bdsc,bscp->spbd", emb.astype(jnp.float32), gathered.astype(jnp.float32)).astype(jnp.bfloat16)
            return jnp.sum(partial_value.astype(jnp.float32), axis=0).reshape(PROBES, BLK_DEV * BS)

        total = lax.map(one_shard, (blocks, lists))
        total = jnp.moveaxis(total, 0, 1).reshape(PROBES, NDOC)
        return total * quality[None, :] - vec

    first = apply(probes)
    second = 2.0 * apply(first) - probes
    return first, second
```

```python
import functools

import jax
import jax.numpy as jnp
from jax import lax
from jax.experimental import pallas as pl
from jax.experimental.pallas import tpu as pltpu
from jax.sharding import PartitionSpec as P

MESH = pl.DeviceIdType.MESH
NY = 4
CH = 16
F32 = jnp.float32
BF16 = jnp.bfloat16


def kernel(nz, ny, ncol, blk, knn, nch, idx_ref, req_ref, emb_ref, q_ref, v_ref, first_ref, second_ref, *scratch):
    scratch = list(scratch)
    nset = 2 * nch
    deep = nz // 2
    half = blk // 2
    piece = blk // ncol
    slots = [[scratch.pop(0) for _ in range(nz)] for _ in range(nset)]
    stage = [scratch.pop(0) for _ in range(nset)]
    table = [scratch.pop(0) for _ in range(nset)]
    part = [scratch.pop(0) for _ in range(nset)]
    recv = [scratch.pop(0) for _ in range(nset)]
    mine = [scratch.pop(0) for _ in range(nset)]
    full = [scratch.pop(0) for _ in range(nset)]
    ask_vmem, ask, z_send, z_recv, y_send, y_recv, x_send, x_recv, ask_send, ask_recv, ask_sem = scratch

    row, col = lax.axis_index("row"), lax.axis_index("col")
    z, y = row // ny, row % ny
    up = (lax.rem(z + 1, nz) * ny + y, col)
    down = (lax.rem(z + nz - 1, nz) * ny + y, col)

    def mate(m):
        return (z * ny + lax.rem(y + m, ny), col)

    def peer(r):
        return lax.rem(col + r, ncol)

    barrier = pltpu.get_barrier_semaphore()
    partners = [up, down] + [mate(m) for m in range(1, ny)] + [(row, peer(r)) for r in range(1, ncol)]
    for device in partners:
        pl.semaphore_signal(barrier, inc=1, device_id=device, device_id_type=MESH)
    pl.semaphore_wait(barrier, len(partners))

    def ask_copy(r):
        return pltpu.make_async_remote_copy(
            src_ref=req_ref.at[r], dst_ref=ask_vmem.at[ny - r],
            send_sem=ask_send.at[r], recv_sem=ask_recv.at[ny - r],
            device_id=mate(r), device_id_type=MESH)

    for r in range(1, ny):
        ask_copy(r).start()
    ask_vmem[0] = req_ref[0]

    def block(b):
        return pl.ds(pl.multiple_of(b * 128, 128), 128)

    def rows_of(n):
        return pl.ds((n % nch) * CH, CH)

    def sums(n, b, weights):
        value = jnp.dot(weights, emb_ref[block(b), :], preferred_element_type=F32).astype(BF16)
        slots[n][0][b] = value
        table[n][ny * nz * 8 + b] = value

    def first_sums(n):
        def body(g, carry):
            for i in range(8):
                b = g * 8 + i
                scaled = (v_ref[rows_of(n), block(b)] * q_ref[pl.ds(b, 1), :]).astype(BF16)
                sums(n, b, scaled)
            return carry

        lax.fori_loop(0, blk // 8, body, 0)

    def slot_of(d, upward):
        if d == 0:
            return 0
        return nz - 1 if d == deep else (2 * d - 1 if upward else 2 * d)

    def z_copy(n, d, k, upward):
        h = k if upward else 1 - k
        part_of = pl.ds(h * half, half)
        sem = ((d - 1) * 2 + k) * 2 + int(upward)
        return pltpu.make_async_remote_copy(
            src_ref=slots[n][slot_of(d - 1, upward)].at[part_of],
            dst_ref=slots[n][slot_of(d, upward)].at[part_of],
            send_sem=z_send.at[n, sem], recv_sem=z_recv.at[n, sem],
            device_id=up if upward else down, device_id_type=MESH)

    def z_start(n, d, k):
        if d < deep or (d == deep and k == 0):
            for upward in (True, False):
                z_copy(n, d, k, upward).start()

    def z_wait(n, d, k):
        for upward in (True, False):
            z_copy(n, d, k, upward).wait_recv()

    def group(d):
        if d == 0:
            return (0,)
        return (nz - 1,) if d == deep else (2 * d - 1, 2 * d)

    def y_stage(n, d):
        ps = group(d)

        def body(t, carry):
            for p in ps:
                for m in range(ny):
                    value = slots[n][p][ask[m, 0, p * 8 + t]]
                    if m == 0:
                        table[n][p * 8 + t] = value
                    else:
                        stage[n][((m - 1) * nz + p) * 8 + t] = value
            return carry

        lax.fori_loop(0, 8, body, 0)
        rows = len(ps) * 8
        for m in range(1, ny):
            pltpu.make_async_remote_copy(
                src_ref=stage[n].at[pl.ds(((m - 1) * nz + ps[0]) * 8, rows)],
                dst_ref=table[n].at[pl.ds(((ny - m) * nz + ps[0]) * 8, rows)],
                send_sem=y_send.at[n], recv_sem=y_recv.at[n],
                device_id=mate(m), device_id_type=MESH).start()

    def y_all(n):
        return pltpu.make_async_remote_copy(
            src_ref=stage[n], dst_ref=table[n].at[pl.ds(nz * 8, (ny - 1) * nz * 8)],
            send_sem=y_send.at[n], recv_sem=y_recv.at[n],
            device_id=mate(1), device_id_type=MESH)

    def partial_piece(n, j):
        for i in range(piece):
            b = j * piece + i
            total = table[n][idx_ref[b * knn]].astype(F32)
            for k in range(1, knn):
                total += table[n][idx_ref[b * knn + k]].astype(F32)
            value = lax.dot_general(total.astype(BF16), emb_ref[block(b), :], (((1,), (1,)), ((), ())),
                                    preferred_element_type=F32)
            part[n][b] = value.astype(BF16)

    def scatter_copy(n, r):
        return pltpu.make_async_remote_copy(
            src_ref=part[n].at[pl.ds(peer(r) * piece, piece)],
            dst_ref=recv[n].at[pl.ds((r - 1) * piece, piece)],
            send_sem=x_send.at[n, 0], recv_sem=x_recv.at[n, 0],
            device_id=(row, peer(r)), device_id_type=MESH)

    def scatter_all(n):
        return pltpu.make_async_remote_copy(
            src_ref=part[n].at[pl.ds(0, (ncol - 1) * piece)], dst_ref=recv[n],
            send_sem=x_send.at[n, 0], recv_sem=x_recv.at[n, 0],
            device_id=(row, peer(1)), device_id_type=MESH)

    def gather_copy(n, r):
        return pltpu.make_async_remote_copy(
            src_ref=mine[n], dst_ref=full[n].at[pl.ds(col * piece, piece)],
            send_sem=x_send.at[n, 1], recv_sem=x_recv.at[n, 1],
            device_id=(row, peer(r)), device_id_type=MESH)

    def gather_all(n):
        return pltpu.make_async_remote_copy(
            src_ref=recv[n], dst_ref=full[n].at[pl.ds(0, (ncol - 1) * piece)],
            send_sem=x_send.at[n, 1], recv_sem=x_recv.at[n, 1],
            device_id=(row, peer(1)), device_id_type=MESH)

    def post_a(n):
        y_all(n).wait_recv()

        def body(r, carry):
            partial_piece(n, peer(r))
            scatter_copy(n, r).start()
            return carry

        lax.fori_loop(1, ncol, body, 0)
        partial_piece(n, col)

    def post_b(n):
        scatter_all(n).wait_recv()
        for i in range(piece):
            total = part[n][col * piece + i].astype(F32)
            for r in range(1, ncol):
                total += recv[n][(r - 1) * piece + i].astype(F32)
            total = total.astype(BF16)
            mine[n][i] = total
            full[n][col * piece + i] = total
        for r in range(1, ncol):
            gather_copy(n, r).start()

    def post_c(n):
        gather_all(n).wait_recv()

        def body(g, carry):
            for i in range(8):
                b = g * 8 + i
                quality = q_ref[pl.ds(b, 1), :]
                value = v_ref[rows_of(n), block(b)]
                total = full[n][b].astype(F32) * quality
                if n < nch:
                    first = total - value
                    first_ref[rows_of(n), block(b)] = first
                    sums(n + nch, b, (first * quality).astype(BF16))
                else:
                    second_ref[rows_of(n), block(b)] = 2.0 * (total - first_ref[rows_of(n), block(b)]) - value
            return carry

        lax.fori_loop(0, blk // 8, body, 0)

    def begin(n):
        z_start(n, 1, 0)
        z_start(n, 1, 1)
        y_stage(n, 0)

    first_sums(0)
    z_start(0, 1, 0)
    z_start(0, 1, 1)
    for n in range(1, nch):
        first_sums(n)
    for r in range(1, ny):
        ask_copy(r).wait_recv()
    to_smem = pltpu.make_async_copy(ask_vmem, ask, ask_sem)
    to_smem.start()
    to_smem.wait()
    y_stage(0, 0)

    events = [(d, k) for d in range(1, deep) for k in (0, 1)]
    for n in range(nset):
        posts = {0: post_a, min(2, len(events) - 1): post_b}
        for e, (d, k) in enumerate(events):
            z_wait(n, d, k)
            z_start(n, d + 1, k)
            if k == 1:
                y_stage(n, d)
            if n > 0:
                if e == 0:
                    post_a(n - 1)
                if e == min(2, len(events) - 1):
                    post_b(n - 1)
                if e == min(4, len(events) - 1):
                    post_c(n - 1)
        if n + 1 < nset:
            begin(n + 1)
        z_wait(n, deep, 0)
        y_stage(n, deep)
    post_a(nset - 1)
    post_b(nset - 1)
    post_c(nset - 1)

    for r in range(1, ny):
        ask_copy(r).wait_send()
    for n in range(nset):
        for d in range(1, deep + 1):
            for k in (0, 1):
                if d < deep or k == 0:
                    for upward in (True, False):
                        z_copy(n, d, k, upward).wait_send()
        y_all(n).wait_send()
        scatter_all(n).wait_send()
        gather_all(n).wait_send()


def tables(neighbors, nz, ny):
    blk, knn = neighbors.shape
    row = lax.axis_index("row")
    z, y = row // ny, row % ny
    flat = neighbors.reshape(-1)
    owner, local = flat // blk, flat % blk
    order = jnp.arange(blk * knn, dtype=jnp.int32)
    before = (owner[:, None] == owner[None, :]) & (order[:, None] < order[None, :])
    rank = jnp.sum(before.astype(jnp.int32), axis=0)
    delta = (owner // ny - z + nz) % nz
    r = (owner % ny - y + ny) % ny
    p = jnp.where(delta < nz // 2, 2 * delta, 2 * (nz - delta) - 1)
    key = jnp.where((owner != row) & (rank < 8), (r * nz + p) * 8 + rank, ny * nz * 8)
    index = jnp.where(owner == row, ny * nz * 8 + local, key)
    hit = key[:, None] == jnp.arange(ny * nz * 8, dtype=jnp.int32)[None, :]
    request = jnp.sum(jnp.where(hit, local[:, None], 0), axis=0).reshape(ny, 1, nz * 8)
    request = jnp.pad(request, ((0, 0), (0, 7), (0, 128 - nz * 8)))
    return index, request


def body(embeddings, quality, probes, neighbors, ny=NY, ncol=8, nz=8):
    blk, knn = neighbors.shape
    nch = probes.shape[0] // CH
    nset = 2 * nch
    piece = blk // ncol
    index, request = tables(neighbors, nz, ny)

    def blocks(count):
        return [pltpu.VMEM((count, CH, 128), BF16)] * nset

    vmem = pl.BlockSpec(memory_space=pltpu.VMEM)
    return pl.pallas_call(
        functools.partial(kernel, nz, ny, ncol, blk, knn, nch),
        out_shape=[jax.ShapeDtypeStruct(probes.shape, F32)] * 2,
        in_specs=[pl.BlockSpec(memory_space=pltpu.SMEM), vmem, vmem, vmem, vmem],
        out_specs=[vmem, vmem],
        scratch_shapes=blocks(blk) * nz
        + blocks((ny - 1) * nz * 8)
        + blocks(ny * nz * 8 + blk)
        + blocks(blk)
        + blocks((ncol - 1) * piece)
        + blocks(piece)
        + blocks(blk)
        + [
            pltpu.VMEM((ny, 8, 128), jnp.int32),
            pltpu.SMEM((ny, 8, 128), jnp.int32),
            pltpu.SemaphoreType.DMA((nset, 2 * nz)),
            pltpu.SemaphoreType.DMA((nset, 2 * nz)),
            pltpu.SemaphoreType.DMA((nset,)),
            pltpu.SemaphoreType.DMA((nset,)),
            pltpu.SemaphoreType.DMA((nset, 2)),
            pltpu.SemaphoreType.DMA((nset, 2)),
            pltpu.SemaphoreType.DMA((ny,)),
            pltpu.SemaphoreType.DMA((ny,)),
            pltpu.SemaphoreType.DMA,
        ],
        compiler_params=pltpu.CompilerParams(
            collective_id=0, has_side_effects=True, vmem_limit_bytes=56 * 1024 * 1024),
    )(index, request, embeddings, quality.reshape(blk, 128), probes)


def solution(mesh):
    placed = (P("row", "col"), P("row"), P(None, "row"), P("row", None))
    return jax.shard_map(
        lambda *arrays: tuple(body(*arrays)),
        mesh=mesh,
        in_specs=placed,
        out_specs=(P(None, "row"), P(None, "row")),
        check_vma=False,
    )
```

```python
import functools

import jax
import jax.numpy as jnp
from jax import lax
from jax.experimental import pallas as pl
from jax.experimental.pallas import tpu as pltpu
from jax.sharding import PartitionSpec as P

MESH = pl.DeviceIdType.MESH
NY = 4
CH = 16
F32 = jnp.float32
BF16 = jnp.bfloat16


def kernel(nz, ny, ncol, blk, knn, nch, idx_ref, req_ref, emb_hbm, q_hbm, v_hbm, total1_ref, total2_ref, *scratch):
    scratch = list(scratch)
    nset = 2 * nch
    deep = nz // 2
    half = blk // 2
    piece = blk // ncol
    slots = [[scratch.pop(0) for _ in range(nz)] for _ in range(nset)]
    stage = [scratch.pop(0) for _ in range(nset)]
    table = [scratch.pop(0) for _ in range(nset)]
    part = [scratch.pop(0) for _ in range(nset)]
    recv = [scratch.pop(0) for _ in range(nset)]
    mine = [scratch.pop(0) for _ in range(nset)]
    full = [scratch.pop(0) for _ in range(nset)]
    emb_ref, q_ref, v_ref, load_sem, ask_vmem, ask, z_send, z_recv, y_send, y_recv, x_send, x_recv, ask_send, ask_recv, ask_sem = scratch

    loads = [pltpu.make_async_copy(src, dst, load_sem.at[i])
             for i, (src, dst) in enumerate(((v_hbm, v_ref), (q_hbm, q_ref), (emb_hbm, emb_ref)))]
    for load in loads:
        load.start()

    row, col = lax.axis_index("row"), lax.axis_index("col")
    z, y = row // ny, row % ny
    up = (lax.rem(z + 1, nz) * ny + y, col)
    down = (lax.rem(z + nz - 1, nz) * ny + y, col)

    def mate(m):
        return (z * ny + lax.rem(y + m, ny), col)

    def peer(r):
        return lax.rem(col + r, ncol)

    barrier = pltpu.get_barrier_semaphore()
    partners = [up, down] + [mate(m) for m in range(1, ny)] + [(row, peer(r)) for r in range(1, ncol)]
    for device in partners:
        pl.semaphore_signal(barrier, inc=1, device_id=device, device_id_type=MESH)

    def ask_copy(r):
        return pltpu.make_async_remote_copy(
            src_ref=req_ref.at[r], dst_ref=ask_vmem.at[ny - r],
            send_sem=ask_send.at[r], recv_sem=ask_recv.at[ny - r],
            device_id=mate(r), device_id_type=MESH)

    ask_vmem[0] = req_ref[0]

    def block(b):
        return pl.ds(pl.multiple_of(b * 128, 128), 128)

    def rows_of(n):
        return pl.ds((n % nch) * CH, CH)

    def sums(n, b, weights):
        value = jnp.dot(weights, emb_ref[block(b), :], preferred_element_type=F32).astype(BF16)
        slots[n][0][b] = value
        table[n][ny * nz * 8 + b] = value

    def first_sums(n):
        def body(g, carry):
            for i in range(8):
                b = g * 8 + i
                scaled = (v_ref[rows_of(n), block(b)] * q_ref[pl.ds(b, 1), :]).astype(BF16)
                sums(n, b, scaled)
            return carry

        lax.fori_loop(0, blk // 8, body, 0)

    def slot_of(d, upward):
        if d == 0:
            return 0
        return nz - 1 if d == deep else (2 * d - 1 if upward else 2 * d)

    def z_copy(n, d, k, upward):
        h = k if upward else 1 - k
        part_of = pl.ds(h * half, half)
        sem = ((d - 1) * 2 + k) * 2 + int(upward)
        return pltpu.make_async_remote_copy(
            src_ref=slots[n][slot_of(d - 1, upward)].at[part_of],
            dst_ref=slots[n][slot_of(d, upward)].at[part_of],
            send_sem=z_send.at[n, sem], recv_sem=z_recv.at[n, sem],
            device_id=up if upward else down, device_id_type=MESH)

    def z_start(n, d, k):
        if d < deep or (d == deep and k == 0):
            for upward in (True, False):
                z_copy(n, d, k, upward).start()

    def z_wait(n, d, k):
        for upward in (True, False):
            z_copy(n, d, k, upward).wait_recv()

    def group(d):
        if d == 0:
            return (0,)
        return (nz - 1,) if d == deep else (2 * d - 1, 2 * d)

    def y_stage(n, d):
        ps = group(d)

        def body(t, carry):
            for p in ps:
                for m in range(ny):
                    value = slots[n][p][ask[m, 0, p * 8 + t]]
                    if m == 0:
                        table[n][p * 8 + t] = value
                    else:
                        stage[n][((m - 1) * nz + p) * 8 + t] = value
            return carry

        lax.fori_loop(0, 8, body, 0)
        rows = len(ps) * 8
        for m in range(1, ny):
            pltpu.make_async_remote_copy(
                src_ref=stage[n].at[pl.ds(((m - 1) * nz + ps[0]) * 8, rows)],
                dst_ref=table[n].at[pl.ds(((ny - m) * nz + ps[0]) * 8, rows)],
                send_sem=y_send.at[n], recv_sem=y_recv.at[n],
                device_id=mate(m), device_id_type=MESH).start()

    def y_all(n):
        return pltpu.make_async_remote_copy(
            src_ref=stage[n], dst_ref=table[n].at[pl.ds(nz * 8, (ny - 1) * nz * 8)],
            send_sem=y_send.at[n], recv_sem=y_recv.at[n],
            device_id=mate(1), device_id_type=MESH)

    def partial_piece(n, j):
        for i in range(piece):
            b = j * piece + i
            total = table[n][idx_ref[b * knn]].astype(F32)
            for k in range(1, knn):
                total += table[n][idx_ref[b * knn + k]].astype(F32)
            value = lax.dot_general(total.astype(BF16), emb_ref[block(b), :], (((1,), (1,)), ((), ())),
                                    preferred_element_type=F32)
            part[n][b] = value.astype(BF16)

    def scatter_copy(n, r):
        return pltpu.make_async_remote_copy(
            src_ref=part[n].at[pl.ds(peer(r) * piece, piece)],
            dst_ref=recv[n].at[pl.ds((r - 1) * piece, piece)],
            send_sem=x_send.at[n, 0], recv_sem=x_recv.at[n, 0],
            device_id=(row, peer(r)), device_id_type=MESH)

    def scatter_all(n):
        return pltpu.make_async_remote_copy(
            src_ref=part[n].at[pl.ds(0, (ncol - 1) * piece)], dst_ref=recv[n],
            send_sem=x_send.at[n, 0], recv_sem=x_recv.at[n, 0],
            device_id=(row, peer(1)), device_id_type=MESH)

    def gather_copy(n, r):
        return pltpu.make_async_remote_copy(
            src_ref=mine[n], dst_ref=full[n].at[pl.ds(col * piece, piece)],
            send_sem=x_send.at[n, 1], recv_sem=x_recv.at[n, 1],
            device_id=(row, peer(r)), device_id_type=MESH)

    def gather_all(n):
        return pltpu.make_async_remote_copy(
            src_ref=recv[n], dst_ref=full[n].at[pl.ds(0, (ncol - 1) * piece)],
            send_sem=x_send.at[n, 1], recv_sem=x_recv.at[n, 1],
            device_id=(row, peer(1)), device_id_type=MESH)

    def post_a(n):
        y_all(n).wait_recv()

        def body(r, carry):
            partial_piece(n, peer(r))
            scatter_copy(n, r).start()
            return carry

        lax.fori_loop(1, ncol, body, 0)
        partial_piece(n, col)

    def post_b(n):
        scatter_all(n).wait_recv()
        for i in range(piece):
            total = part[n][col * piece + i].astype(F32)
            for r in range(1, ncol):
                total += recv[n][(r - 1) * piece + i].astype(F32)
            total = total.astype(BF16)
            mine[n][i] = total
            full[n][col * piece + i] = total
        for r in range(1, ncol):
            gather_copy(n, r).start()

    def post_c(n):
        gather_all(n).wait_recv()

        def body(g, carry):
            for i in range(8):
                b = g * 8 + i
                quality = q_ref[pl.ds(b, 1), :]
                value = v_ref[rows_of(n), block(b)]
                total = full[n][b].astype(F32) * quality
                if n < nch:
                    total1_ref[rows_of(n), block(b)] = full[n][b]
                    sums(n + nch, b, ((total - value) * quality).astype(BF16))
                else:
                    total2_ref[rows_of(n), block(b)] = full[n][b]
            return carry

        lax.fori_loop(0, blk // 8, body, 0)

    for load in loads:
        load.wait()
    first_sums(0)
    pl.semaphore_wait(barrier, len(partners))
    z_start(0, 1, 0)
    z_start(0, 1, 1)
    for r in range(1, ny):
        ask_copy(r).start()
    for n in range(1, nch):
        first_sums(n)
    for r in range(1, ny):
        ask_copy(r).wait_recv()
    to_smem = pltpu.make_async_copy(ask_vmem, ask, ask_sem)
    to_smem.start()
    to_smem.wait()
    y_stage(0, 0)

    events = [(d, k) for d in range(1, deep) for k in (0, 1)]
    last = len(events) - 1
    for n in range(nset):
        for e, (d, k) in enumerate(events):
            z_wait(n, d, k)
            z_start(n, d + 1, k)
            if k == 1:
                y_stage(n, d)
            if n > 0:
                if e == 0:
                    y_stage(n, 0)
                    post_a(n - 1)
                if e == min(2, last):
                    post_b(n - 1)
                if e == min(4, last):
                    post_c(n - 1)
            if e == min(4, last) and n + 1 < nset:
                z_start(n + 1, 1, 0)
                z_start(n + 1, 1, 1)
        z_wait(n, deep, 0)
        y_stage(n, deep)
    post_a(nset - 1)
    post_b(nset - 1)
    post_c(nset - 1)

    for r in range(1, ny):
        ask_copy(r).wait_send()
    for n in range(nset):
        for d in range(1, deep + 1):
            for k in (0, 1):
                if d < deep or k == 0:
                    for upward in (True, False):
                        z_copy(n, d, k, upward).wait_send()
        y_all(n).wait_send()
        scatter_all(n).wait_send()
        gather_all(n).wait_send()


def tables(neighbors, nz, ny):
    blk, knn = neighbors.shape
    row = lax.axis_index("row")
    z, y = row // ny, row % ny
    flat = neighbors.reshape(-1)
    owner, local = flat // blk, flat % blk
    order = jnp.arange(blk * knn, dtype=jnp.int32)
    before = (owner[:, None] == owner[None, :]) & (order[:, None] < order[None, :])
    rank = jnp.sum(before.astype(jnp.int32), axis=0)
    delta = (owner // ny - z + nz) % nz
    r = (owner % ny - y + ny) % ny
    p = jnp.where(delta < nz // 2, 2 * delta, 2 * (nz - delta) - 1)
    key = jnp.where((owner != row) & (rank < 8), (r * nz + p) * 8 + rank, ny * nz * 8)
    index = jnp.where(owner == row, ny * nz * 8 + local, key)
    hit = key[:, None] == jnp.arange(ny * nz * 8, dtype=jnp.int32)[None, :]
    request = jnp.sum(jnp.where(hit, local[:, None], 0), axis=0).reshape(ny, 1, nz * 8)
    request = jnp.pad(request, ((0, 0), (0, 7), (0, 128 - nz * 8)))
    return index, request


def body(embeddings, quality, probes, neighbors, ny=NY, ncol=8, nz=8):
    blk, knn = neighbors.shape
    nch = probes.shape[0] // CH
    nset = 2 * nch
    piece = blk // ncol
    index, request = tables(neighbors, nz, ny)

    def blocks(count):
        return [pltpu.VMEM((count, CH, 128), BF16)] * nset

    hbm = pl.BlockSpec(memory_space=pltpu.HBM)
    vmem = pl.BlockSpec(memory_space=pltpu.VMEM)
    total1, total2 = pl.pallas_call(
        functools.partial(kernel, nz, ny, ncol, blk, knn, nch),
        out_shape=[jax.ShapeDtypeStruct(probes.shape, BF16)] * 2,
        in_specs=[pl.BlockSpec(memory_space=pltpu.SMEM), vmem, hbm, hbm, hbm],
        out_specs=[vmem, vmem],
        scratch_shapes=blocks(blk) * nz
        + blocks((ny - 1) * nz * 8)
        + blocks(ny * nz * 8 + blk)
        + blocks(blk)
        + blocks((ncol - 1) * piece)
        + blocks(piece)
        + blocks(blk)
        + [
            pltpu.VMEM(embeddings.shape, BF16),
            pltpu.VMEM((blk, 128), F32),
            pltpu.VMEM(probes.shape, F32),
            pltpu.SemaphoreType.DMA((3,)),
            pltpu.VMEM((ny, 8, 128), jnp.int32),
            pltpu.SMEM((ny, 8, 128), jnp.int32),
            pltpu.SemaphoreType.DMA((nset, 2 * nz)),
            pltpu.SemaphoreType.DMA((nset, 2 * nz)),
            pltpu.SemaphoreType.DMA((nset,)),
            pltpu.SemaphoreType.DMA((nset,)),
            pltpu.SemaphoreType.DMA((nset, 2)),
            pltpu.SemaphoreType.DMA((nset, 2)),
            pltpu.SemaphoreType.DMA((ny,)),
            pltpu.SemaphoreType.DMA((ny,)),
            pltpu.SemaphoreType.DMA,
        ],
        compiler_params=pltpu.CompilerParams(
            collective_id=0, has_side_effects=True, vmem_limit_bytes=58 * 1024 * 1024),
    )(index, request, embeddings, quality.reshape(blk, 128), probes)
    first = total1.astype(F32) * quality[None, :] - probes
    second = 2.0 * (total2.astype(F32) * quality[None, :] - first) - probes
    return first, second


def solution(mesh):
    placed = (P("row", "col"), P("row"), P(None, "row"), P("row", None))
    return jax.shard_map(
        body,
        mesh=mesh,
        in_specs=placed,
        out_specs=(P(None, "row"), P(None, "row")),
        check_vma=False,
    )
```

```python
import functools

import jax
import jax.numpy as jnp
from jax import lax
from jax.experimental import pallas as pl
from jax.experimental.pallas import tpu as pltpu
from jax.sharding import PartitionSpec as P

MESH = pl.DeviceIdType.MESH
NY = 4
CH = 16
F32 = jnp.float32
BF16 = jnp.bfloat16


def kernel(nz, ny, ncol, blk, knn, nch, near_hbm, emb_hbm, q_hbm, v_hbm, total1_ref, total2_ref, *scratch):
    scratch = list(scratch)
    nset = 2 * nch
    deep = nz // 2
    half = blk // 2
    piece = blk // ncol
    quart = piece // 2
    slots = [[scratch.pop(0) for _ in range(nz)] for _ in range(nset)]
    stage = [scratch.pop(0) for _ in range(nset)]
    table = [scratch.pop(0) for _ in range(nset)]
    part = [scratch.pop(0) for _ in range(nset)]
    recv = [scratch.pop(0) for _ in range(nset)]
    mine = [scratch.pop(0) for _ in range(nset)]
    full = [scratch.pop(0) for _ in range(nset)]
    near_ref, turned, emb_ref, q_ref, v_ref, load_sem, wide, idx_vmem, idx, ask_vmem, ask, z_send, z_recv, y_send, y_recv, x_send, x_recv, ask_send, ask_recv, ask_sem = scratch

    step = emb_ref.shape[0] // 4
    pairs = [(q_hbm, q_ref), (v_hbm.at[0:CH], v_ref.at[0:CH])]
    pairs += [(emb_hbm.at[pl.ds(i * step, step)], emb_ref.at[pl.ds(i * step, step)]) for i in range(4)]
    pairs += [(v_hbm.at[CH:], v_ref.at[CH:]), (near_hbm, near_ref)]
    loads = [pltpu.make_async_copy(src, dst, load_sem.at[i]) for i, (src, dst) in enumerate(pairs)]
    for load in loads:
        load.start()

    row, col = lax.axis_index("row"), lax.axis_index("col")
    z, y = row // ny, row % ny
    up = (lax.rem(z + 1, nz) * ny + y, col)
    down = (lax.rem(z + nz - 1, nz) * ny + y, col)

    def mate(m):
        return (z * ny + lax.rem(y + m, ny), col)

    x, core = col // 2, col % 2
    others = [(dx, dc) for dx in (2, 1, 3) for dc in (0, 1)] + [(0, 1)]

    def peer(dx, dc):
        return lax.rem(x + dx, 4) * 2 + lax.rem(core + dc, 2)

    def place(dx, dc):
        return lax.rem(4 - dx, 4) * 2 + dc - 1

    barrier = pltpu.get_barrier_semaphore()
    partners = [up, down] + [mate(m) for m in range(1, ny)] + [(row, peer(*o)) for o in others]
    for device in partners:
        pl.semaphore_signal(barrier, inc=1, device_id=device, device_id_type=MESH)

    def make_tables():
        i32 = jnp.int32
        wide[...] = jnp.full(wide.shape, -1, i32)
        wide[:, 0:blk] = near_ref[...]
        ids = wide[...]
        owner, local = ids >> (blk.bit_length() - 1), ids & (blk - 1)
        delta = ((owner >> (ny.bit_length() - 1)) - z + nz) & (nz - 1)
        r = ((owner & (ny - 1)) - y + ny) & (ny - 1)
        p = jnp.where(delta < deep, 2 * delta, 2 * (nz - delta) - 1)
        own = owner == row
        start = jnp.where(own, ny * nz * 8 + local, (r * nz + p) * 8)
        shape = (nz * ny, 128)
        sub, lane = lax.broadcasted_iota(i32, shape, 0), lax.broadcasted_iota(i32, shape, 1)
        seen = jnp.zeros(shape, i32)
        picks = [jnp.zeros(shape, i32) for _ in range(8)]
        for k in range(knn):
            hit = jnp.where(sub == jnp.broadcast_to(owner[k:k + 1], shape), 1, 0)
            upto = hit
            shift = 1
            while shift < blk:
                upto = upto + jnp.where(lane >= shift, pltpu.roll(upto, shift, 1), 0)
                shift *= 2
            rank = jnp.sum(hit * (upto - hit + seen), axis=0, keepdims=True)
            seen = seen + jnp.broadcast_to(upto[:, blk - 1:blk], shape)
            idx_vmem[k:k + 1, :] = start[k:k + 1] + jnp.where(own[k:k + 1], 0, jnp.minimum(rank, 7))
            named = hit * jnp.broadcast_to(local[k:k + 1], shape)
            for t in range(8):
                picks[t] = picks[t] + jnp.where(jnp.broadcast_to(rank, shape) == t, named, 0)
        asked = jnp.zeros(shape, i32)
        for t in range(8):
            asked = jnp.where(lane == t, jnp.sum(picks[t], axis=1, keepdims=True), asked)
        asked = jnp.concatenate([asked, jnp.zeros((128 - nz * ny, 128), i32)], axis=0)
        ask_vmem[0] = jnp.transpose(asked)[0:8]

    def ask_copy(r):
        return pltpu.make_async_remote_copy(
            src_ref=ask_vmem.at[0], dst_ref=ask_vmem.at[ny - r],
            send_sem=ask_send.at[r], recv_sem=ask_recv.at[ny - r],
            device_id=mate(r), device_id_type=MESH)

    def block(b):
        return pl.ds(pl.multiple_of(b * 128, 128), 128)

    def rows_of(n):
        return pl.ds((n % nch) * CH, CH)

    def sums(n, b, weights):
        value = jnp.dot(weights, emb_ref[block(b), :], preferred_element_type=F32).astype(BF16)
        slots[n][0][b] = value
        table[n][ny * nz * 8 + b] = value

    def first_sums(n):
        def body(g, carry):
            for i in range(8):
                b = g * 8 + i
                scaled = (v_ref[rows_of(n), block(b)] * q_ref[pl.ds(b, 1), :]).astype(BF16)
                sums(n, b, scaled)
            return carry

        for i in range(4):
            if n == 0:
                loads[2 + i].wait()
            lax.fori_loop(i * blk // 32, (i + 1) * blk // 32, body, 0)

    def slot_of(d, upward):
        if d == 0:
            return 0
        return nz - 1 if d == deep else (2 * d - 1 if upward else 2 * d)

    def z_copy(n, d, k, upward):
        h = k if upward else 1 - k
        part_of = pl.ds(h * half, half)
        sem = ((d - 1) * 2 + k) * 2 + int(upward)
        return pltpu.make_async_remote_copy(
            src_ref=slots[n][slot_of(d - 1, upward)].at[part_of],
            dst_ref=slots[n][slot_of(d, upward)].at[part_of],
            send_sem=z_send.at[n, sem], recv_sem=z_recv.at[n, sem],
            device_id=up if upward else down, device_id_type=MESH)

    def z_start(n, d, k):
        if d < deep or (d == deep and k == 0):
            for upward in (True, False):
                z_copy(n, d, k, upward).start()

    def z_wait(n, d, k):
        for upward in (True, False):
            z_copy(n, d, k, upward).wait_recv()

    def group(d):
        if d == 0:
            return (0,)
        return (nz - 1,) if d == deep else (2 * d - 1, 2 * d)

    def owner_of(p):
        step = nz - (p + 1) // 2 if p % 2 else p // 2
        return lax.rem(z + step, nz) * ny + y

    def y_stage(n, d):
        ps = group(d)

        def body(t, carry):
            for p in ps:
                for m in range(ny):
                    value = slots[n][p][ask[m, t, owner_of(p)]]
                    if m == 0:
                        table[n][p * 8 + t] = value
                    else:
                        stage[n][((m - 1) * nz + p) * 8 + t] = value
            return carry

        lax.fori_loop(0, 8, body, 0)
        rows = len(ps) * 8
        for m in range(1, ny):
            pltpu.make_async_remote_copy(
                src_ref=stage[n].at[pl.ds(((m - 1) * nz + ps[0]) * 8, rows)],
                dst_ref=table[n].at[pl.ds(((ny - m) * nz + ps[0]) * 8, rows)],
                send_sem=y_send.at[n], recv_sem=y_recv.at[n],
                device_id=mate(m), device_id_type=MESH).start()

    def y_all(n):
        return pltpu.make_async_remote_copy(
            src_ref=stage[n], dst_ref=table[n].at[pl.ds(nz * 8, (ny - 1) * nz * 8)],
            send_sem=y_send.at[n], recv_sem=y_recv.at[n],
            device_id=mate(1), device_id_type=MESH)

    def turn(first_block, count):
        def body(g, carry):
            for i in range(4):
                b = first_block + g * 4 + i
                turned[block(b), :] = jnp.transpose(emb_ref[block(b), :])
            return carry

        lax.fori_loop(0, count // 4, body, 0)

    def partial_rows(n, first_block):
        for i in range(quart):
            b = first_block + i
            total = table[n][idx[0, b]].astype(F32)
            for k in range(1, knn):
                total += table[n][idx[k, b]].astype(F32)
            part[n][b] = jnp.dot(total.astype(BF16), turned[block(b), :], preferred_element_type=F32).astype(BF16)

    def scatter_copy(n, h, dx, dc):
        return pltpu.make_async_remote_copy(
            src_ref=part[n].at[pl.ds(peer(dx, dc) * piece + h * quart, quart)],
            dst_ref=recv[n].at[pl.ds(place(dx, dc) * piece + h * quart, quart)],
            send_sem=x_send.at[n, h], recv_sem=x_recv.at[n, h],
            device_id=(row, peer(dx, dc)), device_id_type=MESH)

    def gather_copy(n, h, dx, dc):
        return pltpu.make_async_remote_copy(
            src_ref=mine[n].at[pl.ds(h * quart, quart)],
            dst_ref=full[n].at[pl.ds(col * piece + h * quart, quart)],
            send_sem=x_send.at[n, 2 + h], recv_sem=x_recv.at[n, 2 + h],
            device_id=(row, peer(dx, dc)), device_id_type=MESH)

    def x_all(n, sem):
        rows = pl.ds(0, (ncol - 1) * quart)
        return pltpu.make_async_remote_copy(
            src_ref=part[n].at[rows], dst_ref=(recv[n] if sem < 2 else full[n]).at[rows],
            send_sem=x_send.at[n, sem], recv_sem=x_recv.at[n, sem],
            device_id=(row, peer(0, 1)), device_id_type=MESH)

    def post_a(n, h):
        if h == 0:
            y_all(n).wait_recv()

        def body(i, carry):
            dx = jnp.where(i == 0, 2, jnp.where(i == 1, 1, 3))
            for dc in (0, 1):
                partial_rows(n, peer(dx, dc) * piece + h * quart)
            for dc in (0, 1):
                scatter_copy(n, h, dx, dc).start()
            return carry

        lax.fori_loop(0, 3, body, 0)
        partial_rows(n, peer(0, 1) * piece + h * quart)
        partial_rows(n, col * piece + h * quart)
        scatter_copy(n, h, 0, 1).start()

    def post_b(n, h):
        x_all(n, h).wait_recv()
        for i in range(h * quart, (h + 1) * quart):
            total = part[n][col * piece + i].astype(F32)
            for r in range(1, ncol):
                total += recv[n][(r - 1) * piece + i].astype(F32)
            total = total.astype(BF16)
            mine[n][i] = total
            full[n][col * piece + i] = total
        for dx, dc in others:
            gather_copy(n, h, dx, dc).start()

    def post_c(n):
        for h in (0, 1):
            x_all(n, 2 + h).wait_recv()

        def body(g, carry):
            for i in range(8):
                b = g * 8 + i
                quality = q_ref[pl.ds(b, 1), :]
                value = v_ref[rows_of(n), block(b)]
                total = full[n][b].astype(F32) * quality
                if n < nch:
                    total1_ref[rows_of(n), block(b)] = full[n][b]
                    sums(n + nch, b, ((total - value) * quality).astype(BF16))
                else:
                    total2_ref[rows_of(n), block(b)] = full[n][b]
            return carry

        lax.fori_loop(0, blk // 8, body, 0)

    for load in loads[:2]:
        load.wait()
    first_sums(0)
    for load in loads[6:]:
        load.wait()
    pl.semaphore_wait(barrier, len(partners))
    z_start(0, 1, 0)
    z_start(0, 1, 1)
    make_tables()
    for r in range(1, ny):
        ask_copy(r).start()
    for n in range(1, nch):
        first_sums(n)
    to_smem = [pltpu.make_async_copy(idx_vmem, idx, ask_sem.at[0]), pltpu.make_async_copy(ask_vmem, ask, ask_sem.at[1])]

    events = [(d, k) for d in range(1, deep) for k in (0, 1)]
    for n in range(nset):
        for e, (d, k) in enumerate(events):
            z_wait(n, d, k)
            z_start(n, d + 1, k)
            if n == 0 and e == 0:
                for r in range(1, ny):
                    ask_copy(r).wait_recv()
                for copy in to_smem:
                    copy.start()
            if n == 0 and e == 1:
                for copy in to_smem:
                    copy.wait()
                y_stage(0, 0)
            if k == 1:
                y_stage(n, d)
            if n == 0 and e < 4:
                turn(e * blk // 4, blk // 4)
            if n > 0:
                if e == 0:
                    y_stage(n, 0)
                    post_a(n - 1, 0)
                if e == 1:
                    post_a(n - 1, 1)
                    post_b(n - 1, 0)
                if e == 2:
                    post_b(n - 1, 1)
                if e == 4:
                    post_c(n - 1)
            if e == 4 and n + 1 < nset:
                z_start(n + 1, 1, 0)
                z_start(n + 1, 1, 1)
        z_wait(n, deep, 0)
        y_stage(n, deep)
    post_a(nset - 1, 0)
    post_a(nset - 1, 1)
    post_b(nset - 1, 0)
    post_b(nset - 1, 1)
    post_c(nset - 1)

    for r in range(1, ny):
        ask_copy(r).wait_send()
    for n in range(nset):
        for d in range(1, deep + 1):
            for k in (0, 1):
                if d < deep or k == 0:
                    for upward in (True, False):
                        z_copy(n, d, k, upward).wait_send()
        y_all(n).wait_send()
        for sem in range(4):
            x_all(n, sem).wait_send()


def body(embeddings, quality, probes, neighbors, ny=NY, ncol=8, nz=8):
    blk, knn = neighbors.shape
    nch = probes.shape[0] // CH
    nset = 2 * nch
    piece = blk // ncol

    def blocks(count):
        return [pltpu.VMEM((count, CH, 128), BF16)] * nset

    hbm = pl.BlockSpec(memory_space=pltpu.HBM)
    vmem = pl.BlockSpec(memory_space=pltpu.VMEM)
    total1, total2 = pl.pallas_call(
        functools.partial(kernel, nz, ny, ncol, blk, knn, nch),
        out_shape=[jax.ShapeDtypeStruct(probes.shape, BF16)] * 2,
        in_specs=[hbm] * 4,
        out_specs=[vmem, vmem],
        scratch_shapes=blocks(blk) * nz
        + blocks((ny - 1) * nz * 8)
        + blocks(ny * nz * 8 + blk)
        + blocks(blk)
        + blocks((ncol - 1) * piece)
        + blocks(piece)
        + blocks(blk)
        + [
            pltpu.VMEM((knn, blk), jnp.int32),
            pltpu.VMEM(embeddings.shape, BF16),
            pltpu.VMEM(embeddings.shape, BF16),
            pltpu.VMEM((blk, 128), F32),
            pltpu.VMEM(probes.shape, F32),
            pltpu.SemaphoreType.DMA((8,)),
            pltpu.VMEM((knn, 128), jnp.int32),
            pltpu.VMEM((knn, 128), jnp.int32),
            pltpu.SMEM((knn, 128), jnp.int32),
            pltpu.VMEM((ny, 8, 128), jnp.int32),
            pltpu.SMEM((ny, 8, 128), jnp.int32),
            pltpu.SemaphoreType.DMA((nset, 2 * nz)),
            pltpu.SemaphoreType.DMA((nset, 2 * nz)),
            pltpu.SemaphoreType.DMA((nset,)),
            pltpu.SemaphoreType.DMA((nset,)),
            pltpu.SemaphoreType.DMA((nset, 4)),
            pltpu.SemaphoreType.DMA((nset, 4)),
            pltpu.SemaphoreType.DMA((ny,)),
            pltpu.SemaphoreType.DMA((ny,)),
            pltpu.SemaphoreType.DMA((2,)),
        ],
        compiler_params=pltpu.CompilerParams(
            collective_id=0, has_side_effects=True, vmem_limit_bytes=36 * 1024 * 1024),
    )(*[pltpu.with_memory_space_constraint(array, pltpu.HBM)
        for array in (neighbors.T, embeddings, quality.reshape(blk, 128), probes)])
    first = total1.astype(F32) * quality[None, :] - probes
    second = 2.0 * (total2.astype(F32) * quality[None, :] - first) - probes
    return first, second


def solution(mesh):
    placed = (P("row", "col"), P("row"), P(None, "row"), P("row", None))
    return jax.shard_map(
        body,
        mesh=mesh,
        in_specs=placed,
        out_specs=(P(None, "row"), P(None, "row")),
        check_vma=False,
    )
```

```python
import functools

import jax
import jax.numpy as jnp
from jax import lax
from jax.experimental import pallas as pl
from jax.experimental.pallas import tpu as pltpu
from jax.sharding import PartitionSpec as P

MESH = pl.DeviceIdType.MESH
NY = 4
CH = 16
F32 = jnp.float32
BF16 = jnp.bfloat16


def kernel(nz, ny, ncol, blk, knn, nch, near_hbm, emb_hbm, q_hbm, v_hbm, total1_out, total2_out, *scratch):
    scratch = list(scratch)
    nset = 2 * nch
    deep = nz // 2
    half = blk // 2
    piece = blk // ncol
    quart = piece // 2
    slots = [[scratch.pop(0) for _ in range(nz)] for _ in range(nset)]
    stage = [scratch.pop(0) for _ in range(nset)]
    table = [scratch.pop(0) for _ in range(nset)]
    part = [scratch.pop(0) for _ in range(nset)]
    recv = [scratch.pop(0) for _ in range(nset)]
    mine = [scratch.pop(0) for _ in range(nset)]
    full = [scratch.pop(0) for _ in range(nset)]
    total1_ref, total2_ref, out_sem, near_ref, turned, emb_ref, q_ref, v_ref, load_sem, wide, idx_vmem, idx, ask_vmem, ask, z_send, z_recv, y_send, y_recv, x_send, x_recv, ask_send, ask_recv, ask_sem = scratch

    step = emb_ref.shape[0] // 4
    quarters = (0, 2, 1, 3)
    pairs = [(q_hbm, q_ref)]
    for i in quarters:
        docs = pl.ds(i * step, step)
        pairs += [(v_hbm.at[0:CH, docs], v_ref.at[0:CH, docs]), (emb_hbm.at[docs], emb_ref.at[docs])]
    pairs += [(v_hbm.at[CH:], v_ref.at[CH:]), (near_hbm, near_ref)]
    loads = [pltpu.make_async_copy(src, dst, load_sem.at[i]) for i, (src, dst) in enumerate(pairs)]
    for load in loads:
        load.start()

    row, col = lax.axis_index("row"), lax.axis_index("col")
    z, y = row // ny, row % ny
    up = (lax.rem(z + 1, nz) * ny + y, col)
    down = (lax.rem(z + nz - 1, nz) * ny + y, col)

    def mate(m):
        return (z * ny + lax.rem(y + m, ny), col)

    x, core = col // 2, col % 2
    others = [(dx, dc) for dx in (2, 1, 3) for dc in (0, 1)] + [(0, 1)]

    def peer(dx, dc):
        return lax.rem(x + dx, 4) * 2 + lax.rem(core + dc, 2)

    def place(dx, dc):
        return lax.rem(4 - dx, 4) * 2 + dc - 1

    barrier = pltpu.get_barrier_semaphore()
    partners = [up, down] + [mate(m) for m in range(1, ny)] + [(row, peer(*o)) for o in others]
    for device in partners:
        pl.semaphore_signal(barrier, inc=1, device_id=device, device_id_type=MESH)

    def make_tables():
        i32 = jnp.int32
        wide[...] = jnp.full(wide.shape, -1, i32)
        wide[:, 0:blk] = near_ref[...]
        ids = wide[...]
        owner, local = ids >> (blk.bit_length() - 1), ids & (blk - 1)
        delta = ((owner >> (ny.bit_length() - 1)) - z + nz) & (nz - 1)
        r = ((owner & (ny - 1)) - y + ny) & (ny - 1)
        p = jnp.where(delta < deep, 2 * delta, 2 * (nz - delta) - 1)
        own = owner == row
        start = jnp.where(own, ny * nz * 8 + local, (r * nz + p) * 8)
        shape = (nz * ny, 128)
        sub, lane = lax.broadcasted_iota(i32, shape, 0), lax.broadcasted_iota(i32, shape, 1)
        seen = jnp.zeros(shape, i32)
        picks = [jnp.zeros(shape, i32) for _ in range(8)]
        for k in range(knn):
            hit = jnp.where(sub == jnp.broadcast_to(owner[k:k + 1], shape), 1, 0)
            upto = hit
            shift = 1
            while shift < blk:
                upto = upto + jnp.where(lane >= shift, pltpu.roll(upto, shift, 1), 0)
                shift *= 2
            rank = jnp.sum(hit * (upto - hit + seen), axis=0, keepdims=True)
            seen = seen + jnp.broadcast_to(upto[:, blk - 1:blk], shape)
            idx_vmem[k:k + 1, :] = start[k:k + 1] + jnp.where(own[k:k + 1], 0, jnp.minimum(rank, 7))
            named = hit * jnp.broadcast_to(local[k:k + 1], shape)
            for t in range(8):
                picks[t] = picks[t] + jnp.where(jnp.broadcast_to(rank, shape) == t, named, 0)
        asked = jnp.zeros(shape, i32)
        for t in range(8):
            asked = jnp.where(lane == t, jnp.sum(picks[t], axis=1, keepdims=True), asked)
        asked = jnp.concatenate([asked, jnp.zeros((128 - nz * ny, 128), i32)], axis=0)
        ask_vmem[0] = jnp.transpose(asked)[0:8]

    def ask_copy(r):
        return pltpu.make_async_remote_copy(
            src_ref=ask_vmem.at[0], dst_ref=ask_vmem.at[ny - r],
            send_sem=ask_send.at[r], recv_sem=ask_recv.at[ny - r],
            device_id=mate(r), device_id_type=MESH)

    def block(b):
        return pl.ds(pl.multiple_of(b * 128, 128), 128)

    def rows_of(n):
        return pl.ds((n % nch) * CH, CH)

    def sums(n, b, weights):
        value = jnp.dot(weights, emb_ref[block(b), :], preferred_element_type=F32).astype(BF16)
        slots[n][0][b] = value
        table[n][ny * nz * 8 + b] = value

    def first_sums(n, i):
        def body(g, carry):
            for j in range(8):
                b = g * 8 + j
                scaled = (v_ref[rows_of(n), block(b)] * q_ref[pl.ds(b, 1), :]).astype(BF16)
                sums(n, b, scaled)
            return carry

        lax.fori_loop(i * blk // 32, (i + 1) * blk // 32, body, 0)

    def slot_of(d, upward):
        if d == 0:
            return 0
        return nz - 1 if d == deep else (2 * d - 1 if upward else 2 * d)

    def z_copy(n, d, k, upward, first, count, sem):
        rows = pl.ds((k if upward else 1 - k) * half + first, count)
        return pltpu.make_async_remote_copy(
            src_ref=slots[n][slot_of(d - 1, upward)].at[rows],
            dst_ref=slots[n][slot_of(d, upward)].at[rows],
            send_sem=z_send.at[n, sem], recv_sem=z_recv.at[n, sem],
            device_id=up if upward else down, device_id_type=MESH)

    def z_parts(n, d, k, upward):
        sem = ((d - 1) * 2 + k) * 2 + int(upward)
        if (n, d, k) == (0, 1, 0):
            return [z_copy(n, d, k, upward, 0, half // 2, sem),
                    z_copy(n, d, k, upward, half // 2, half // 2, 14 + int(upward))]
        return [z_copy(n, d, k, upward, 0, half, sem)]

    def z_start(n, d, k):
        if d < deep or (d == deep and k == 0):
            for upward in (True, False):
                for copy in z_parts(n, d, k, upward):
                    copy.start()

    def z_wait(n, d, k):
        for upward in (True, False):
            for copy in z_parts(n, d, k, upward):
                copy.wait_recv()

    def group(d):
        if d == 0:
            return (0,)
        return (nz - 1,) if d == deep else (2 * d - 1, 2 * d)

    def owner_of(p):
        step = nz - (p + 1) // 2 if p % 2 else p // 2
        return lax.rem(z + step, nz) * ny + y

    def y_stage(n, d):
        ps = group(d)

        def body(t, carry):
            for p in ps:
                for m in range(ny):
                    value = slots[n][p][ask[m, t, owner_of(p)]]
                    if m == 0:
                        table[n][p * 8 + t] = value
                    else:
                        stage[n][((m - 1) * nz + p) * 8 + t] = value
            return carry

        lax.fori_loop(0, 8, body, 0)
        rows = len(ps) * 8
        for m in (2, 1, 3):
            pltpu.make_async_remote_copy(
                src_ref=stage[n].at[pl.ds(((m - 1) * nz + ps[0]) * 8, rows)],
                dst_ref=table[n].at[pl.ds(((ny - m) * nz + ps[0]) * 8, rows)],
                send_sem=y_send.at[n], recv_sem=y_recv.at[n],
                device_id=mate(m), device_id_type=MESH).start()

    def y_all(n):
        return pltpu.make_async_remote_copy(
            src_ref=stage[n], dst_ref=table[n].at[pl.ds(nz * 8, (ny - 1) * nz * 8)],
            send_sem=y_send.at[n], recv_sem=y_recv.at[n],
            device_id=mate(1), device_id_type=MESH)

    def turn(first_block, count):
        def body(g, carry):
            for i in range(4):
                b = first_block + g * 4 + i
                turned[block(b), :] = jnp.transpose(emb_ref[block(b), :])
            return carry

        lax.fori_loop(0, count // 4, body, 0)

    def partial_rows(n, first_block):
        for i in range(quart):
            b = first_block + i
            total = table[n][idx[0, b]].astype(F32)
            for k in range(1, knn):
                total += table[n][idx[k, b]].astype(F32)
            part[n][b] = jnp.dot(total.astype(BF16), turned[block(b), :], preferred_element_type=F32).astype(BF16)

    def scatter_copy(n, h, dx, dc):
        return pltpu.make_async_remote_copy(
            src_ref=part[n].at[pl.ds(peer(dx, dc) * piece + h * quart, quart)],
            dst_ref=recv[n].at[pl.ds(place(dx, dc) * piece + h * quart, quart)],
            send_sem=x_send.at[n, h], recv_sem=x_recv.at[n, h],
            device_id=(row, peer(dx, dc)), device_id_type=MESH)

    def gather_copy(n, h, dx, dc):
        return pltpu.make_async_remote_copy(
            src_ref=mine[n].at[pl.ds(h * quart, quart)],
            dst_ref=full[n].at[pl.ds(col * piece + h * quart, quart)],
            send_sem=x_send.at[n, 2 + h], recv_sem=x_recv.at[n, 2 + h],
            device_id=(row, peer(dx, dc)), device_id_type=MESH)

    def x_all(n, sem):
        rows = pl.ds(0, (ncol - 1) * quart)
        return pltpu.make_async_remote_copy(
            src_ref=part[n].at[rows], dst_ref=(recv[n] if sem < 2 else full[n]).at[rows],
            send_sem=x_send.at[n, sem], recv_sem=x_recv.at[n, sem],
            device_id=(row, peer(0, 1)), device_id_type=MESH)

    def post_a(n, h):
        if h == 0:
            y_all(n).wait_recv()

        def body(i, carry):
            dx = jnp.where(i == 0, 2, jnp.where(i == 1, 1, 3))
            for dc in (0, 1):
                partial_rows(n, peer(dx, dc) * piece + h * quart)
            for dc in (0, 1):
                scatter_copy(n, h, dx, dc).start()
            return carry

        lax.fori_loop(0, 3, body, 0)
        partial_rows(n, peer(0, 1) * piece + h * quart)
        partial_rows(n, col * piece + h * quart)
        scatter_copy(n, h, 0, 1).start()

    def post_b(n, h):
        x_all(n, h).wait_recv()
        for i in range(h * quart, (h + 1) * quart):
            total = part[n][col * piece + i].astype(F32)
            for r in range(1, ncol):
                total += recv[n][(r - 1) * piece + i].astype(F32)
            total = total.astype(BF16)
            mine[n][i] = total
            full[n][col * piece + i] = total
        for dx, dc in others:
            gather_copy(n, h, dx, dc).start()

    def out_copy(n):
        source, target = (total1_ref, total1_out) if n < nch else (total2_ref, total2_out)
        return pltpu.make_async_copy(source.at[rows_of(n)], target.at[rows_of(n)], out_sem.at[n])

    def post_c(n):
        for h in (0, 1):
            x_all(n, 2 + h).wait_recv()

        def body(g, carry):
            for i in range(8):
                b = g * 8 + i
                quality = q_ref[pl.ds(b, 1), :]
                value = v_ref[rows_of(n), block(b)]
                total = full[n][b].astype(F32) * quality
                if n < nch:
                    total1_ref[rows_of(n), block(b)] = full[n][b]
                    sums(n + nch, b, ((total - value) * quality).astype(BF16))
                else:
                    total2_ref[rows_of(n), block(b)] = full[n][b]
            return carry

        lax.fori_loop(0, blk // 8, body, 0)
        out_copy(n).start()

    loads[0].wait()
    for turn_of, i in enumerate(quarters):
        loads[1 + 2 * turn_of].wait()
        loads[2 + 2 * turn_of].wait()
        first_sums(0, i)
        if turn_of == 0:
            pl.semaphore_wait(barrier, len(partners))
        z_parts(0, 1, 0, i < 2)[i % 2].start()
    z_start(0, 1, 1)
    for load in loads[9:]:
        load.wait()
    make_tables()
    for r in range(1, ny):
        ask_copy(r).start()
    for n in range(1, nch):
        for i in range(4):
            first_sums(n, i)
    to_smem = [pltpu.make_async_copy(idx_vmem, idx, ask_sem.at[0]), pltpu.make_async_copy(ask_vmem, ask, ask_sem.at[1])]

    def sent(n):
        for d in range(1, deep + 1):
            for k in (0, 1):
                if d < deep or k == 0:
                    for upward in (True, False):
                        for copy in z_parts(n, d, k, upward):
                            copy.wait_send()
        y_all(n).wait_send()
        for sem in range(4):
            x_all(n, sem).wait_send()
        out_copy(n).wait()

    events = [(d, k) for d in range(1, deep) for k in (0, 1)]
    for n in range(nset):
        for e, (d, k) in enumerate(events):
            z_wait(n, d, k)
            z_start(n, d + 1, k)
            if n == 0 and e == 0:
                for r in range(1, ny):
                    ask_copy(r).wait_recv()
                for copy in to_smem:
                    copy.start()
            if n == 0 and e == 1:
                for copy in to_smem:
                    copy.wait()
                y_stage(0, 0)
            if k == 1:
                y_stage(n, d)
            if n == 0 and e < 4:
                turn(e * blk // 4, blk // 4)
            if n > 0:
                if e == 0:
                    y_stage(n, 0)
                if e == 1:
                    post_a(n - 1, 0)
                    post_a(n - 1, 1)
                if e == (3 if n == nset - 1 else 2):
                    post_b(n - 1, 0)
                    post_b(n - 1, 1)
                if e == (5 if n == nset - 1 else 4):
                    post_c(n - 1)
            if e == 4 and n + 1 < nset:
                z_start(n + 1, 1, 0)
                z_start(n + 1, 1, 1)
        z_wait(n, deep, 0)
        y_stage(n, deep)
        if n > 0:
            sent(n - 1)
    post_a(nset - 1, 0)
    post_a(nset - 1, 1)
    post_b(nset - 1, 0)
    post_b(nset - 1, 1)
    post_c(nset - 1)

    for r in range(1, ny):
        ask_copy(r).wait_send()
    sent(nset - 1)


def body(embeddings, quality, probes, neighbors, ny=NY, ncol=8, nz=8):
    blk, knn = neighbors.shape
    nch = probes.shape[0] // CH
    nset = 2 * nch
    piece = blk // ncol

    def blocks(count):
        return [pltpu.VMEM((count, CH, 128), BF16)] * nset

    hbm = pl.BlockSpec(memory_space=pltpu.HBM)
    total1, total2 = pl.pallas_call(
        functools.partial(kernel, nz, ny, ncol, blk, knn, nch),
        out_shape=[jax.ShapeDtypeStruct(probes.shape, BF16)] * 2,
        in_specs=[hbm] * 4,
        out_specs=[pl.BlockSpec(memory_space=pl.ANY)] * 2,
        scratch_shapes=blocks(blk) * nz
        + blocks((ny - 1) * nz * 8)
        + blocks(ny * nz * 8 + blk)
        + blocks(blk)
        + blocks((ncol - 1) * piece)
        + blocks(piece)
        + blocks(blk)
        + [
            pltpu.VMEM(probes.shape, BF16),
            pltpu.VMEM(probes.shape, BF16),
            pltpu.SemaphoreType.DMA((nset,)),
            pltpu.VMEM((knn, blk), jnp.int32),
            pltpu.VMEM(embeddings.shape, BF16),
            pltpu.VMEM(embeddings.shape, BF16),
            pltpu.VMEM((blk, 128), F32),
            pltpu.VMEM(probes.shape, F32),
            pltpu.SemaphoreType.DMA((11,)),
            pltpu.VMEM((knn, 128), jnp.int32),
            pltpu.VMEM((knn, 128), jnp.int32),
            pltpu.SMEM((knn, 128), jnp.int32),
            pltpu.VMEM((ny, 8, 128), jnp.int32),
            pltpu.SMEM((ny, 8, 128), jnp.int32),
            pltpu.SemaphoreType.DMA((nset, 2 * nz)),
            pltpu.SemaphoreType.DMA((nset, 2 * nz)),
            pltpu.SemaphoreType.DMA((nset,)),
            pltpu.SemaphoreType.DMA((nset,)),
            pltpu.SemaphoreType.DMA((nset, 4)),
            pltpu.SemaphoreType.DMA((nset, 4)),
            pltpu.SemaphoreType.DMA((ny,)),
            pltpu.SemaphoreType.DMA((ny,)),
            pltpu.SemaphoreType.DMA((2,)),
        ],
        compiler_params=pltpu.CompilerParams(
            collective_id=0, has_side_effects=True, vmem_limit_bytes=36 * 1024 * 1024),
    )(*[pltpu.with_memory_space_constraint(array, pltpu.HBM)
        for array in (neighbors.T, embeddings, quality.reshape(blk, 128), probes)])
    first = total1.astype(F32) * quality[None, :] - probes
    second = 2.0 * (total2.astype(F32) * quality[None, :] - first) - probes
    return first, second


def solution(mesh):
    placed = (P("row", "col"), P("row"), P(None, "row"), P("row", None))
    return jax.shard_map(
        body,
        mesh=mesh,
        in_specs=placed,
        out_specs=(P(None, "row"), P(None, "row")),
        check_vma=False,
    )
```

```python
import functools

import jax
import jax.numpy as jnp
from jax import lax
from jax.experimental import pallas as pl
from jax.experimental.pallas import tpu as pltpu
from jax.sharding import PartitionSpec as P

MESH = pl.DeviceIdType.MESH
NY = 4
CH = 16
F32 = jnp.float32
BF16 = jnp.bfloat16


def kernel(nz, ny, ncol, blk, knn, nch, near_hbm, emb_hbm, q_hbm, v_hbm, total1_out, total2_out, *scratch):
    scratch = list(scratch)
    nset = 2 * nch
    deep = nz // 2
    half = blk // 2
    piece = blk // ncol
    quart = piece // 2
    slots = [[scratch.pop(0) for _ in range(nz)] for _ in range(nset)]
    stage = [scratch.pop(0) for _ in range(nset)]
    table = [scratch.pop(0) for _ in range(nset)]
    part = [scratch.pop(0) for _ in range(nset)]
    recv = [scratch.pop(0) for _ in range(nset)]
    mine = [scratch.pop(0) for _ in range(nset)]
    full = [scratch.pop(0) for _ in range(nset)]
    total1_ref, total2_ref, out_sem, near_ref, turned, emb_ref, q_ref, v_ref, load_sem, wide, idx_vmem, idx, ask_vmem, ask, z_send, z_recv, y_send, y_recv, x_send, x_recv, p_send, p_recv, ask_send, ask_recv, ask_sem = scratch

    step = emb_ref.shape[0] // 4
    quarters = (0, 2, 1, 3)
    pairs = [(q_hbm, q_ref)]
    for i in quarters:
        docs = pl.ds(i * step, step)
        pairs += [(v_hbm.at[0:CH, docs], v_ref.at[0:CH, docs]), (emb_hbm.at[docs], emb_ref.at[docs])]
    pairs += [(v_hbm.at[CH:], v_ref.at[CH:]), (near_hbm, near_ref)]
    loads = [pltpu.make_async_copy(src, dst, load_sem.at[i]) for i, (src, dst) in enumerate(pairs)]
    for load in loads:
        load.start()

    row, col = lax.axis_index("row"), lax.axis_index("col")
    z, y = row // ny, row % ny
    up = (lax.rem(z + 1, nz) * ny + y, col)
    down = (lax.rem(z + nz - 1, nz) * ny + y, col)

    def mate(m):
        return (z * ny + lax.rem(y + m, ny), col)

    x, core = col // 2, col % 2
    others = [(dx, dc) for dx in (2, 1, 3) for dc in (0, 1)] + [(0, 1)]

    def peer(dx, dc):
        return lax.rem(x + dx, 4) * 2 + lax.rem(core + dc, 2)

    def place(dx, dc):
        return lax.rem(4 - dx, 4) * 2 + dc - 1

    barrier = pltpu.get_barrier_semaphore()
    partners = [up, down] + [mate(m) for m in range(1, ny)] + [(row, peer(*o)) for o in others]
    for device in partners:
        pl.semaphore_signal(barrier, inc=1, device_id=device, device_id_type=MESH)

    def make_tables():
        i32 = jnp.int32
        wide[...] = jnp.full(wide.shape, -1, i32)
        wide[:, 0:blk] = near_ref[...]
        ids = wide[...]
        owner, local = ids >> (blk.bit_length() - 1), ids & (blk - 1)
        delta = ((owner >> (ny.bit_length() - 1)) - z + nz) & (nz - 1)
        r = ((owner & (ny - 1)) - y + ny) & (ny - 1)
        p = jnp.where(delta < deep, 2 * delta, 2 * (nz - delta) - 1)
        own = owner == row
        start = jnp.where(own, ny * nz * 8 + local, (r * nz + p) * 8)
        shape = (nz * ny, 128)
        sub, lane = lax.broadcasted_iota(i32, shape, 0), lax.broadcasted_iota(i32, shape, 1)
        seen = jnp.zeros(shape, i32)
        picks = [jnp.zeros(shape, i32) for _ in range(8)]
        for k in range(knn):
            hit = jnp.where(sub == jnp.broadcast_to(owner[k:k + 1], shape), 1, 0)
            upto = hit
            shift = 1
            while shift < blk:
                upto = upto + jnp.where(lane >= shift, pltpu.roll(upto, shift, 1), 0)
                shift *= 2
            rank = jnp.sum(hit * (upto - hit + seen), axis=0, keepdims=True)
            seen = seen + jnp.broadcast_to(upto[:, blk - 1:blk], shape)
            idx_vmem[k:k + 1, :] = start[k:k + 1] + jnp.where(own[k:k + 1], 0, jnp.minimum(rank, 7))
            named = hit * jnp.broadcast_to(local[k:k + 1], shape)
            for t in range(8):
                picks[t] = picks[t] + jnp.where(jnp.broadcast_to(rank, shape) == t, named, 0)
        asked = jnp.zeros(shape, i32)
        for t in range(8):
            asked = jnp.where(lane == t, jnp.sum(picks[t], axis=1, keepdims=True), asked)
        asked = jnp.concatenate([asked, jnp.zeros((128 - nz * ny, 128), i32)], axis=0)
        ask_vmem[0] = jnp.transpose(asked)[0:8]

    def ask_copy(r):
        return pltpu.make_async_remote_copy(
            src_ref=ask_vmem.at[0], dst_ref=ask_vmem.at[ny - r],
            send_sem=ask_send.at[r], recv_sem=ask_recv.at[ny - r],
            device_id=mate(r), device_id_type=MESH)

    def block(b):
        return pl.ds(pl.multiple_of(b * 128, 128), 128)

    def rows_of(n):
        return pl.ds((n % nch) * CH, CH)

    def sums(n, b, weights):
        value = jnp.dot(weights, emb_ref[block(b), :], preferred_element_type=F32).astype(BF16)
        slots[n][0][b] = value
        table[n][ny * nz * 8 + b] = value

    def first_sums(n, i):
        def body(g, carry):
            for j in range(8):
                b = g * 8 + j
                scaled = (v_ref[rows_of(n), block(b)] * q_ref[pl.ds(b, 1), :]).astype(BF16)
                sums(n, b, scaled)
            return carry

        lax.fori_loop(i * blk // 32, (i + 1) * blk // 32, body, 0)

    def slot_of(d, upward):
        if d == 0:
            return 0
        return nz - 1 if d == deep else (2 * d - 1 if upward else 2 * d)

    def z_copy(n, d, k, upward, first, count, sem):
        rows = pl.ds((k if upward else 1 - k) * half + first, count)
        return pltpu.make_async_remote_copy(
            src_ref=slots[n][slot_of(d - 1, upward)].at[rows],
            dst_ref=slots[n][slot_of(d, upward)].at[rows],
            send_sem=z_send.at[n, int(upward)], recv_sem=z_recv.at[n % 2, sem],
            device_id=up if upward else down, device_id_type=MESH)

    def z_parts(n, d, k, upward):
        sem = ((d - 1) * 2 + k) * 2 + int(upward)
        if (n, d, k) == (0, 1, 0):
            return [z_copy(n, d, k, upward, 0, half // 2, sem),
                    z_copy(n, d, k, upward, half // 2, half // 2, 14 + int(upward))]
        return [z_copy(n, d, k, upward, 0, half, sem)]

    def z_start(n, d, k):
        if d < deep or (d == deep and k == 0):
            for upward in (True, False):
                for copy in z_parts(n, d, k, upward):
                    copy.start()

    def z_wait(n, d, k):
        for upward in (True, False):
            for copy in z_parts(n, d, k, upward):
                copy.wait_recv()

    def group(d):
        if d == 0:
            return (0,)
        return (nz - 1,) if d == deep else (2 * d - 1, 2 * d)

    def owner_of(p):
        step = nz - (p + 1) // 2 if p % 2 else p // 2
        return lax.rem(z + step, nz) * ny + y

    def y_stage(n, d):
        ps = group(d)

        def body(t, carry):
            for p in ps:
                for m in range(ny):
                    value = slots[n][p][ask[m, t, owner_of(p)]]
                    if m == 0:
                        table[n][p * 8 + t] = value
                    else:
                        stage[n][((m - 1) * nz + p) * 8 + t] = value
            return carry

        lax.fori_loop(0, 8, body, 0)
        rows = len(ps) * 8
        for m in (2, 1, 3):
            pltpu.make_async_remote_copy(
                src_ref=stage[n].at[pl.ds(((m - 1) * nz + ps[0]) * 8, rows)],
                dst_ref=table[n].at[pl.ds(((ny - m) * nz + ps[0]) * 8, rows)],
                send_sem=y_send.at[n], recv_sem=y_recv.at[n],
                device_id=mate(m), device_id_type=MESH).start()

    def y_all(n):
        return pltpu.make_async_remote_copy(
            src_ref=stage[n], dst_ref=table[n].at[pl.ds(nz * 8, (ny - 1) * nz * 8)],
            send_sem=y_send.at[n], recv_sem=y_recv.at[n],
            device_id=mate(1), device_id_type=MESH)

    def turn(first_block, count):
        def body(g, carry):
            for i in range(4):
                b = first_block + g * 4 + i
                turned[block(b), :] = jnp.transpose(emb_ref[block(b), :])
            return carry

        lax.fori_loop(0, count // 4, body, 0)

    def partial_rows(n, first_block):
        for i in range(quart):
            b = first_block + i
            total = table[n][idx[0, b]].astype(F32)
            for k in range(1, knn):
                total += table[n][idx[k, b]].astype(F32)
            part[n][b] = jnp.dot(total.astype(BF16), turned[block(b), :], preferred_element_type=F32).astype(BF16)

    def scatter_copy(n, h, dx, dc):
        return pltpu.make_async_remote_copy(
            src_ref=part[n].at[pl.ds(peer(dx, dc) * piece + h * quart, quart)],
            dst_ref=recv[n].at[pl.ds(place(dx, dc) * piece + h * quart, quart)],
            send_sem=x_send.at[n % 2, h], recv_sem=x_recv.at[n % 2, h],
            device_id=(row, peer(dx, dc)), device_id_type=MESH)

    def gather_copy(n, h, dx, dc):
        return pltpu.make_async_remote_copy(
            src_ref=mine[n].at[pl.ds(h * quart, quart)],
            dst_ref=full[n].at[pl.ds(col * piece + h * quart, quart)],
            send_sem=x_send.at[n % 2, 2 + h], recv_sem=x_recv.at[n % 2, 2 + h],
            device_id=(row, peer(dx, dc)), device_id_type=MESH)

    def x_all(n, sem):
        rows = pl.ds(0, (ncol - 1) * quart)
        return pltpu.make_async_remote_copy(
            src_ref=part[n].at[rows], dst_ref=(recv[n] if sem < 2 else full[n]).at[rows],
            send_sem=x_send.at[n % 2, sem], recv_sem=x_recv.at[n % 2, sem],
            device_id=(row, peer(0, 1)), device_id_type=MESH)

    def ring_copy(n, h, dx):
        return gather_copy(n, h, dx, 0)

    def ring_all(n, h):
        rows = pl.ds(0, 3 * quart)
        return pltpu.make_async_remote_copy(
            src_ref=part[n].at[rows], dst_ref=full[n].at[rows],
            send_sem=x_send.at[n % 2, 2 + h], recv_sem=x_recv.at[n % 2, 2 + h],
            device_id=(row, peer(1, 0)), device_id_type=MESH)

    def pair_copy(n, h, dx):
        rows = pl.ds(peer(dx, 0) * piece + h * quart, quart)
        return pltpu.make_async_remote_copy(
            src_ref=full[n].at[rows] if dx else mine[n].at[pl.ds(h * quart, quart)], dst_ref=full[n].at[rows],
            send_sem=p_send.at[h], recv_sem=p_recv.at[h],
            device_id=(row, peer(0, 1)), device_id_type=MESH)

    def pair_all(n, h):
        rows = pl.ds(0, 4 * quart)
        return pltpu.make_async_remote_copy(
            src_ref=part[n].at[rows], dst_ref=full[n].at[rows],
            send_sem=p_send.at[h], recv_sem=p_recv.at[h],
            device_id=(row, peer(0, 1)), device_id_type=MESH)

    def hand_on(n, h):
        ring_all(n, h).wait_recv()
        for dx in (2, 1, 3):
            pair_copy(n, h, dx).start()

    def post_a(n, h):
        if h == 0:
            y_all(n).wait_recv()

        def body(i, carry):
            dx = jnp.where(i == 0, 2, jnp.where(i == 1, 1, 3))
            for dc in (0, 1):
                partial_rows(n, peer(dx, dc) * piece + h * quart)
            for dc in (0, 1):
                scatter_copy(n, h, dx, dc).start()
            return carry

        lax.fori_loop(0, 3, body, 0)
        partial_rows(n, peer(0, 1) * piece + h * quart)
        partial_rows(n, col * piece + h * quart)
        scatter_copy(n, h, 0, 1).start()

    def post_b(n, h):
        x_all(n, h).wait_recv()
        for i in range(h * quart, (h + 1) * quart):
            total = part[n][col * piece + i].astype(F32)
            for r in range(1, ncol):
                total += recv[n][(r - 1) * piece + i].astype(F32)
            total = total.astype(BF16)
            mine[n][i] = total
            full[n][col * piece + i] = total
        if n == nset - 1:
            for dx in (2, 1, 3):
                ring_copy(n, h, dx).start()
            pair_copy(n, h, 0).start()
        else:
            for dx, dc in others:
                gather_copy(n, h, dx, dc).start()

    def out_copy(n):
        source, target = (total1_ref, total1_out) if n < nch else (total2_ref, total2_out)
        return pltpu.make_async_copy(source.at[rows_of(n)], target.at[rows_of(n)], out_sem.at[n])

    def post_c(n):
        for h in (0, 1):
            (pair_all(n, h) if n == nset - 1 else x_all(n, 2 + h)).wait_recv()

        def body(g, carry):
            for i in range(8):
                b = g * 8 + i
                quality = q_ref[pl.ds(b, 1), :]
                value = v_ref[rows_of(n), block(b)]
                total = full[n][b].astype(F32) * quality
                if n < nch:
                    total1_ref[rows_of(n), block(b)] = full[n][b]
                    sums(n + nch, b, ((total - value) * quality).astype(BF16))
                else:
                    total2_ref[rows_of(n), block(b)] = full[n][b]
            return carry

        lax.fori_loop(0, blk // 8, body, 0)
        out_copy(n).start()

    loads[0].wait()
    for turn_of, i in enumerate(quarters):
        loads[1 + 2 * turn_of].wait()
        loads[2 + 2 * turn_of].wait()
        first_sums(0, i)
        if turn_of == 0:
            pl.semaphore_wait(barrier, len(partners))
        z_parts(0, 1, 0, i < 2)[i % 2].start()
    z_start(0, 1, 1)
    for load in loads[9:]:
        load.wait()
    make_tables()
    for r in range(1, ny):
        ask_copy(r).start()
    for n in range(1, nch):
        for i in range(4):
            first_sums(n, i)
    to_smem = [pltpu.make_async_copy(idx_vmem, idx, ask_sem.at[0]), pltpu.make_async_copy(ask_vmem, ask, ask_sem.at[1])]

    def sent(n):
        for upward in (True, False):
            rows = pl.ds(0, (2 * deep - 1) * half)
            pltpu.make_async_remote_copy(
                src_ref=table[n].at[rows], dst_ref=table[n].at[rows],
                send_sem=z_send.at[n, int(upward)], recv_sem=z_recv.at[n % 2, int(upward)],
                device_id=up if upward else down, device_id_type=MESH).wait_send()
        y_all(n).wait_send()
        for h in (0, 1):
            x_all(n, h).wait_send()
            if n == nset - 1:
                ring_all(n, h).wait_send()
                pair_all(n, h).wait_send()
            else:
                x_all(n, 2 + h).wait_send()
        out_copy(n).wait()

    events = [(d, k) for d in range(1, deep) for k in (0, 1)]
    for n in range(nset):
        for e, (d, k) in enumerate(events):
            z_wait(n, d, k)
            z_start(n, d + 1, k)
            if n == 0 and e == 0:
                for r in range(1, ny):
                    ask_copy(r).wait_recv()
                for copy in to_smem:
                    copy.start()
            if n == 0 and e == 1:
                for copy in to_smem:
                    copy.wait()
                y_stage(0, 0)
            if k == 1:
                y_stage(n, d)
            if n == 0 and e < 4:
                turn(e * blk // 4, blk // 4)
            if n > 0:
                if e == 0:
                    y_stage(n, 0)
                if e == 1:
                    post_a(n - 1, 0)
                    post_a(n - 1, 1)
                if e == (3 if n == nset - 1 else 2):
                    post_b(n - 1, 0)
                    post_b(n - 1, 1)
                if e == (5 if n == nset - 1 else 4):
                    post_c(n - 1)
            if e == 4 and n + 1 < nset:
                z_start(n + 1, 1, 0)
                z_start(n + 1, 1, 1)
        z_wait(n, deep, 0)
        y_stage(n, deep)
        if n > 0:
            sent(n - 1)
    post_a(nset - 1, 0)
    post_a(nset - 1, 1)
    post_b(nset - 1, 0)
    post_b(nset - 1, 1)
    hand_on(nset - 1, 0)
    hand_on(nset - 1, 1)
    post_c(nset - 1)

    for r in range(1, ny):
        ask_copy(r).wait_send()
    sent(nset - 1)


def body(embeddings, quality, probes, neighbors, ny=NY, ncol=8, nz=8):
    blk, knn = neighbors.shape
    nch = probes.shape[0] // CH
    nset = 2 * nch
    piece = blk // ncol

    def blocks(count):
        return [pltpu.VMEM((count, CH, 128), BF16)] * nset

    hbm = pl.BlockSpec(memory_space=pltpu.HBM)
    total1, total2 = pl.pallas_call(
        functools.partial(kernel, nz, ny, ncol, blk, knn, nch),
        out_shape=[jax.ShapeDtypeStruct(probes.shape, BF16)] * 2,
        in_specs=[hbm] * 4,
        out_specs=[pl.BlockSpec(memory_space=pl.ANY)] * 2,
        scratch_shapes=blocks(blk) * nz
        + blocks((ny - 1) * nz * 8)
        + blocks(ny * nz * 8 + blk)
        + blocks(blk)
        + blocks((ncol - 1) * piece)
        + blocks(piece)
        + blocks(blk)
        + [
            pltpu.VMEM(probes.shape, BF16),
            pltpu.VMEM(probes.shape, BF16),
            pltpu.SemaphoreType.DMA((nset,)),
            pltpu.VMEM((knn, blk), jnp.int32),
            pltpu.VMEM(embeddings.shape, BF16),
            pltpu.VMEM(embeddings.shape, BF16),
            pltpu.VMEM((blk, 128), F32),
            pltpu.VMEM(probes.shape, F32),
            pltpu.SemaphoreType.DMA((11,)),
            pltpu.VMEM((knn, 128), jnp.int32),
            pltpu.VMEM((knn, 128), jnp.int32),
            pltpu.SMEM((knn, 128), jnp.int32),
            pltpu.VMEM((ny, 8, 128), jnp.int32),
            pltpu.SMEM((ny, 8, 128), jnp.int32),
            pltpu.SemaphoreType.DMA((nset, 2)),
            pltpu.SemaphoreType.DMA((2, 2 * nz)),
            pltpu.SemaphoreType.DMA((nset,)),
            pltpu.SemaphoreType.DMA((nset,)),
            pltpu.SemaphoreType.DMA((2, 4)),
            pltpu.SemaphoreType.DMA((2, 4)),
            pltpu.SemaphoreType.DMA((2,)),
            pltpu.SemaphoreType.DMA((2,)),
            pltpu.SemaphoreType.DMA((ny,)),
            pltpu.SemaphoreType.DMA((ny,)),
            pltpu.SemaphoreType.DMA((2,)),
        ],
        compiler_params=pltpu.CompilerParams(
            collective_id=0, has_side_effects=True, vmem_limit_bytes=36 * 1024 * 1024),
    )(*[pltpu.with_memory_space_constraint(array, pltpu.HBM)
        for array in (neighbors.T, embeddings, quality.reshape(blk, 128), probes)])
    first = total1.astype(F32) * quality[None, :] - probes
    second = 2.0 * (total2.astype(F32) * quality[None, :] - first) - probes
    return first, second


def solution(mesh):
    placed = (P("row", "col"), P("row"), P(None, "row"), P("row", None))
    return jax.shard_map(
        body,
        mesh=mesh,
        in_specs=placed,
        out_specs=(P(None, "row"), P(None, "row")),
        check_vma=False,
    )
```

```python
import functools

import jax
import jax.numpy as jnp
from jax import lax
from jax.experimental import pallas as pl
from jax.experimental.pallas import tpu as pltpu
from jax.sharding import PartitionSpec as P

MESH = pl.DeviceIdType.MESH
NY = 4
CH = 16
F32 = jnp.float32
BF16 = jnp.bfloat16


def kernel(nz, ny, ncol, blk, knn, nch, near_hbm, emb_hbm, q_hbm, v_hbm, total1_out, total2_out, *scratch):
    scratch = list(scratch)
    nset = 2 * nch
    deep = nz // 2
    half = blk // 2
    piece = blk // ncol
    quart = piece // 2
    slots = [[scratch.pop(0) for _ in range(nz)] for _ in range(nset)]
    stage = [scratch.pop(0) for _ in range(nset)]
    table = [scratch.pop(0) for _ in range(nset)]
    part = [scratch.pop(0) for _ in range(nset)]
    recv = [scratch.pop(0) for _ in range(nset)]
    mine = [scratch.pop(0) for _ in range(nset)]
    full = [scratch.pop(0) for _ in range(nset)]
    total1_ref, total2_ref, out_sem, near_ref, turned, emb_ref, q_ref, v_ref, load_sem, wide, idx_vmem, idx, ask_vmem, ask, z_send, z_recv, y_send, y_recv, x_send, x_recv, p_send, p_recv, ask_send, ask_recv, ask_sem = scratch

    step = emb_ref.shape[0] // 4
    quarters = (0, 2, 1, 3)
    pairs = [(q_hbm, q_ref)]
    for i in quarters:
        docs = pl.ds(i * step, step)
        pairs += [(v_hbm.at[0:CH, docs], v_ref.at[0:CH, docs]), (emb_hbm.at[docs], emb_ref.at[docs])]
    pairs += [(v_hbm.at[CH:], v_ref.at[CH:]), (near_hbm, near_ref)]
    loads = [pltpu.make_async_copy(src, dst, load_sem.at[i]) for i, (src, dst) in enumerate(pairs)]
    for load in loads:
        load.start()

    row, col = lax.axis_index("row"), lax.axis_index("col")
    z, y = row // ny, row % ny
    up = (lax.rem(z + 1, nz) * ny + y, col)
    down = (lax.rem(z + nz - 1, nz) * ny + y, col)

    def mate(m):
        return (z * ny + lax.rem(y + m, ny), col)

    x, core = col // 2, col % 2
    others = [(dx, dc) for dx in (2, 1, 3) for dc in (0, 1)] + [(0, 1)]

    def peer(dx, dc):
        return lax.rem(x + dx, 4) * 2 + lax.rem(core + dc, 2)

    def place(dx, dc):
        return lax.rem(4 - dx, 4) * 2 + dc - 1

    barrier = pltpu.get_barrier_semaphore()
    partners = [up, down] + [mate(m) for m in range(1, ny)] + [(row, peer(*o)) for o in others]
    for device in partners:
        pl.semaphore_signal(barrier, inc=1, device_id=device, device_id_type=MESH)

    def make_tables():
        i32 = jnp.int32
        wide[...] = jnp.full(wide.shape, -1, i32)
        wide[:, 0:blk] = near_ref[...]
        ids = wide[...]
        owner, local = ids >> (blk.bit_length() - 1), ids & (blk - 1)
        delta = ((owner >> (ny.bit_length() - 1)) - z + nz) & (nz - 1)
        r = ((owner & (ny - 1)) - y + ny) & (ny - 1)
        p = jnp.where(delta < deep, 2 * delta, 2 * (nz - delta) - 1)
        own = owner == row
        start = jnp.where(own, ny * nz * 8 + local, (r * nz + p) * 8)
        shape = (nz * ny, 128)
        sub, lane = lax.broadcasted_iota(i32, shape, 0), lax.broadcasted_iota(i32, shape, 1)
        seen = jnp.zeros(shape, i32)
        picks = [jnp.zeros(shape, i32) for _ in range(8)]
        for k in range(knn):
            hit = jnp.where(sub == jnp.broadcast_to(owner[k:k + 1], shape), 1, 0)
            upto = hit
            shift = 1
            while shift < blk:
                upto = upto + jnp.where(lane >= shift, pltpu.roll(upto, shift, 1), 0)
                shift *= 2
            rank = jnp.sum(hit * (upto - hit + seen), axis=0, keepdims=True)
            seen = seen + jnp.broadcast_to(upto[:, blk - 1:blk], shape)
            idx_vmem[k:k + 1, :] = start[k:k + 1] + jnp.where(own[k:k + 1], 0, jnp.minimum(rank, 7))
            named = hit * jnp.broadcast_to(local[k:k + 1], shape)
            for t in range(8):
                picks[t] = picks[t] + jnp.where(jnp.broadcast_to(rank, shape) == t, named, 0)
        asked = jnp.zeros(shape, i32)
        for t in range(8):
            asked = jnp.where(lane == t, jnp.sum(picks[t], axis=1, keepdims=True), asked)
        asked = jnp.concatenate([asked, jnp.zeros((128 - nz * ny, 128), i32)], axis=0)
        ask_vmem[0] = jnp.transpose(asked)[0:8]

    def ask_copy(r):
        return pltpu.make_async_remote_copy(
            src_ref=ask_vmem.at[0], dst_ref=ask_vmem.at[ny - r],
            send_sem=ask_send.at[r], recv_sem=ask_recv.at[ny - r],
            device_id=mate(r), device_id_type=MESH)

    def block(b):
        return pl.ds(pl.multiple_of(b * 128, 128), 128)

    def rows_of(n):
        return pl.ds((n % nch) * CH, CH)

    def sums(n, b, weights):
        value = jnp.dot(weights, emb_ref[block(b), :], preferred_element_type=F32).astype(BF16)
        slots[n][0][b] = value
        table[n][ny * nz * 8 + b] = value

    def first_sums(n, i):
        def body(g, carry):
            for j in range(8):
                b = g * 8 + j
                scaled = (v_ref[rows_of(n), block(b)] * q_ref[pl.ds(b, 1), :]).astype(BF16)
                sums(n, b, scaled)
            return carry

        lax.fori_loop(i * blk // 32, (i + 1) * blk // 32, body, 0)

    def slot_of(d, upward):
        if d == 0:
            return 0
        return nz - 1 if d == deep else (2 * d - 1 if upward else 2 * d)

    def z_copy(n, d, k, upward, first, count, sem):
        rows = pl.ds((k if upward else 1 - k) * half + first, count)
        return pltpu.make_async_remote_copy(
            src_ref=slots[n][slot_of(d - 1, upward)].at[rows],
            dst_ref=slots[n][slot_of(d, upward)].at[rows],
            send_sem=z_send.at[n, int(upward)], recv_sem=z_recv.at[n % 2, sem],
            device_id=up if upward else down, device_id_type=MESH)

    def z_parts(n, d, k, upward):
        sem = ((d - 1) * 2 + k) * 2 + int(upward)
        if (n, d, k) == (0, 1, 0):
            return [z_copy(n, d, k, upward, 0, half // 2, sem),
                    z_copy(n, d, k, upward, half // 2, half // 2, 14 + int(upward))]
        return [z_copy(n, d, k, upward, 0, half, sem)]

    def z_start(n, d, k):
        if d < deep or (d == deep and k == 0):
            for upward in (True, False):
                for copy in z_parts(n, d, k, upward):
                    copy.start()

    def z_wait(n, d, k):
        for upward in (True, False):
            for copy in z_parts(n, d, k, upward):
                copy.wait_recv()

    def group(d):
        if d == 0:
            return (0,)
        return (nz - 1,) if d == deep else (2 * d - 1, 2 * d)

    def owner_of(p):
        step = nz - (p + 1) // 2 if p % 2 else p // 2
        return lax.rem(z + step, nz) * ny + y

    def y_stage(n, d):
        ps = group(d)

        def body(t, carry):
            for p in ps:
                for m in range(ny):
                    value = slots[n][p][ask[m, t, owner_of(p)]]
                    if m == 0:
                        table[n][p * 8 + t] = value
                    else:
                        stage[n][((m - 1) * nz + p) * 8 + t] = value
            return carry

        lax.fori_loop(0, 8, body, 0)
        rows = len(ps) * 8
        for m in (2, 1, 3):
            pltpu.make_async_remote_copy(
                src_ref=stage[n].at[pl.ds(((m - 1) * nz + ps[0]) * 8, rows)],
                dst_ref=table[n].at[pl.ds(((ny - m) * nz + ps[0]) * 8, rows)],
                send_sem=y_send.at[n], recv_sem=y_recv.at[n],
                device_id=mate(m), device_id_type=MESH).start()

    def y_all(n):
        return pltpu.make_async_remote_copy(
            src_ref=stage[n], dst_ref=table[n].at[pl.ds(nz * 8, (ny - 1) * nz * 8)],
            send_sem=y_send.at[n], recv_sem=y_recv.at[n],
            device_id=mate(1), device_id_type=MESH)

    def turn(first_block, count):
        def body(g, carry):
            for i in range(4):
                b = first_block + g * 4 + i
                turned[block(b), :] = jnp.transpose(emb_ref[block(b), :])
            return carry

        lax.fori_loop(0, count // 4, body, 0)

    def partial_rows(n, first_block):
        for i in range(quart):
            b = first_block + i
            total = table[n][idx[0, b]].astype(F32)
            for k in range(1, knn):
                total += table[n][idx[k, b]].astype(F32)
            part[n][b] = jnp.dot(total.astype(BF16), turned[block(b), :], preferred_element_type=F32).astype(BF16)

    def scatter_copy(n, h, dx, dc):
        return pltpu.make_async_remote_copy(
            src_ref=part[n].at[pl.ds(peer(dx, dc) * piece + h * quart, quart)],
            dst_ref=recv[n].at[pl.ds(place(dx, dc) * piece + h * quart, quart)],
            send_sem=x_send.at[n % 2, h], recv_sem=x_recv.at[n % 2, h],
            device_id=(row, peer(dx, dc)), device_id_type=MESH)

    def gather_copy(n, h, dx, dc):
        return pltpu.make_async_remote_copy(
            src_ref=mine[n].at[pl.ds(h * quart, quart)],
            dst_ref=full[n].at[pl.ds(col * piece + h * quart, quart)],
            send_sem=x_send.at[n % 2, 2 + h], recv_sem=x_recv.at[n % 2, 2 + h],
            device_id=(row, peer(dx, dc)), device_id_type=MESH)

    def x_all(n, sem):
        rows = pl.ds(0, (ncol - 1) * quart)
        return pltpu.make_async_remote_copy(
            src_ref=part[n].at[rows], dst_ref=(recv[n] if sem < 2 else full[n]).at[rows],
            send_sem=x_send.at[n % 2, sem], recv_sem=x_recv.at[n % 2, sem],
            device_id=(row, peer(0, 1)), device_id_type=MESH)

    def ring_copy(n, h, dx):
        return gather_copy(n, h, dx, 0)

    def ring_all(n, h):
        rows = pl.ds(0, 3 * quart)
        return pltpu.make_async_remote_copy(
            src_ref=part[n].at[rows], dst_ref=full[n].at[rows],
            send_sem=x_send.at[n % 2, 2 + h], recv_sem=x_recv.at[n % 2, 2 + h],
            device_id=(row, peer(1, 0)), device_id_type=MESH)

    def pair_copy(n, h, dx):
        rows = pl.ds(peer(dx, 0) * piece + h * quart, quart)
        return pltpu.make_async_remote_copy(
            src_ref=full[n].at[rows] if dx else mine[n].at[pl.ds(h * quart, quart)], dst_ref=full[n].at[rows],
            send_sem=p_send.at[h], recv_sem=p_recv.at[h],
            device_id=(row, peer(0, 1)), device_id_type=MESH)

    def pair_all(n, h):
        rows = pl.ds(0, 4 * quart)
        return pltpu.make_async_remote_copy(
            src_ref=part[n].at[rows], dst_ref=full[n].at[rows],
            send_sem=p_send.at[h], recv_sem=p_recv.at[h],
            device_id=(row, peer(0, 1)), device_id_type=MESH)

    def hand_on(n, h):
        ring_all(n, h).wait_recv()
        for dx in (2, 1, 3):
            pair_copy(n, h, dx).start()

    def post_a(n, h):
        if h == 0:
            y_all(n).wait_recv()

        def body(i, carry):
            dx = jnp.where(i == 0, 2, jnp.where(i == 1, 1, 3))
            for dc in (0, 1):
                partial_rows(n, peer(dx, dc) * piece + h * quart)
            for dc in (0, 1):
                scatter_copy(n, h, dx, dc).start()
            return carry

        lax.fori_loop(0, 3, body, 0)
        partial_rows(n, peer(0, 1) * piece + h * quart)
        partial_rows(n, col * piece + h * quart)
        scatter_copy(n, h, 0, 1).start()

    def post_b(n, h):
        x_all(n, h).wait_recv()
        for i in range(h * quart, (h + 1) * quart):
            total = part[n][col * piece + i].astype(F32)
            for r in range(1, ncol):
                total += recv[n][(r - 1) * piece + i].astype(F32)
            total = total.astype(BF16)
            mine[n][i] = total
            full[n][col * piece + i] = total
        if n == nset - 1:
            for dx in (2, 1, 3):
                ring_copy(n, h, dx).start()
            pair_copy(n, h, 0).start()
        else:
            for dx, dc in others:
                gather_copy(n, h, dx, dc).start()

    def out_copy(n):
        source, target = (total1_ref, total1_out) if n < nch else (total2_ref, total2_out)
        return pltpu.make_async_copy(source.at[rows_of(n)], target.at[rows_of(n)], out_sem.at[n])

    def post_c(n):
        for h in (0, 1):
            (pair_all(n, h) if n == nset - 1 else x_all(n, 2 + h)).wait_recv()

        def body(g, carry):
            for i in range(8):
                b = g * 8 + i
                quality = q_ref[pl.ds(b, 1), :]
                value = v_ref[rows_of(n), block(b)]
                total = full[n][b].astype(F32) * quality
                if n < nch:
                    total1_ref[rows_of(n), block(b)] = full[n][b]
                    sums(n + nch, b, ((total - value) * quality).astype(BF16))
                else:
                    total2_ref[rows_of(n), block(b)] = full[n][b]
            return carry

        lax.fori_loop(0, blk // 16, body, 0)
        if n < nch:
            z_parts(n + nch, 1, 0, True)[0].start()
        lax.fori_loop(blk // 16, blk // 8, body, 0)
        if n < nch:
            z_parts(n + nch, 1, 0, False)[0].start()
            z_start(n + nch, 1, 1)
        out_copy(n).start()

    loads[0].wait()
    for turn_of, i in enumerate(quarters):
        loads[1 + 2 * turn_of].wait()
        loads[2 + 2 * turn_of].wait()
        first_sums(0, i)
        if turn_of == 0:
            pl.semaphore_wait(barrier, len(partners))
        z_parts(0, 1, 0, i < 2)[i % 2].start()
    z_start(0, 1, 1)
    for load in loads[9:]:
        load.wait()
    make_tables()
    for r in range(1, ny):
        ask_copy(r).start()
    for n in range(1, nch):
        for i in range(4):
            first_sums(n, i)
    to_smem = [pltpu.make_async_copy(idx_vmem, idx, ask_sem.at[0]), pltpu.make_async_copy(ask_vmem, ask, ask_sem.at[1])]

    def sent(n):
        for upward in (True, False):
            rows = pl.ds(0, (2 * deep - 1) * half)
            pltpu.make_async_remote_copy(
                src_ref=table[n].at[rows], dst_ref=table[n].at[rows],
                send_sem=z_send.at[n, int(upward)], recv_sem=z_recv.at[n % 2, int(upward)],
                device_id=up if upward else down, device_id_type=MESH).wait_send()
        y_all(n).wait_send()
        for h in (0, 1):
            x_all(n, h).wait_send()
            if n == nset - 1:
                ring_all(n, h).wait_send()
                pair_all(n, h).wait_send()
            else:
                x_all(n, 2 + h).wait_send()
        out_copy(n).wait()

    events = [(d, k) for d in range(1, deep) for k in (0, 1)]
    for n in range(nset):
        for e, (d, k) in enumerate(events):
            z_wait(n, d, k)
            z_start(n, d + 1, k)
            if n == 0 and e == 0:
                for r in range(1, ny):
                    ask_copy(r).wait_recv()
                for copy in to_smem:
                    copy.start()
            if n == 0 and e == 1:
                for copy in to_smem:
                    copy.wait()
                y_stage(0, 0)
            if k == 1:
                y_stage(n, d)
            if n == 0 and e < 4:
                turn(e * blk // 4, blk // 4)
            if n > 0:
                if e == 0:
                    y_stage(n, 0)
                if e == 1:
                    post_a(n - 1, 0)
                    post_a(n - 1, 1)
                if e == (3 if n == nset - 1 else 2):
                    post_b(n - 1, 0)
                if e == 3:
                    post_b(n - 1, 1)
                if e == (5 if n == nset - 1 else 4):
                    post_c(n - 1)
            if e == 4 and n + 1 < nch:
                z_start(n + 1, 1, 0)
                z_start(n + 1, 1, 1)
        z_wait(n, deep, 0)
        y_stage(n, deep)
        if n > 0:
            sent(n - 1)
    post_a(nset - 1, 0)
    post_a(nset - 1, 1)
    post_b(nset - 1, 0)
    post_b(nset - 1, 1)
    hand_on(nset - 1, 0)
    hand_on(nset - 1, 1)
    post_c(nset - 1)

    for r in range(1, ny):
        ask_copy(r).wait_send()
    sent(nset - 1)


def body(embeddings, quality, probes, neighbors, ny=NY, ncol=8, nz=8):
    blk, knn = neighbors.shape
    nch = probes.shape[0] // CH
    nset = 2 * nch
    piece = blk // ncol

    def blocks(count):
        return [pltpu.VMEM((count, CH, 128), BF16)] * nset

    hbm = pl.BlockSpec(memory_space=pltpu.HBM)
    total1, total2 = pl.pallas_call(
        functools.partial(kernel, nz, ny, ncol, blk, knn, nch),
        out_shape=[jax.ShapeDtypeStruct(probes.shape, BF16)] * 2,
        in_specs=[hbm] * 4,
        out_specs=[pl.BlockSpec(memory_space=pl.ANY)] * 2,
        scratch_shapes=blocks(blk) * nz
        + blocks((ny - 1) * nz * 8)
        + blocks(ny * nz * 8 + blk)
        + blocks(blk)
        + blocks((ncol - 1) * piece)
        + blocks(piece)
        + blocks(blk)
        + [
            pltpu.VMEM(probes.shape, BF16),
            pltpu.VMEM(probes.shape, BF16),
            pltpu.SemaphoreType.DMA((nset,)),
            pltpu.VMEM((knn, blk), jnp.int32),
            pltpu.VMEM(embeddings.shape, BF16),
            pltpu.VMEM(embeddings.shape, BF16),
            pltpu.VMEM((blk, 128), F32),
            pltpu.VMEM(probes.shape, F32),
            pltpu.SemaphoreType.DMA((11,)),
            pltpu.VMEM((knn, 128), jnp.int32),
            pltpu.VMEM((knn, 128), jnp.int32),
            pltpu.SMEM((knn, 128), jnp.int32),
            pltpu.VMEM((ny, 8, 128), jnp.int32),
            pltpu.SMEM((ny, 8, 128), jnp.int32),
            pltpu.SemaphoreType.DMA((nset, 2)),
            pltpu.SemaphoreType.DMA((2, 2 * nz)),
            pltpu.SemaphoreType.DMA((nset,)),
            pltpu.SemaphoreType.DMA((nset,)),
            pltpu.SemaphoreType.DMA((2, 4)),
            pltpu.SemaphoreType.DMA((2, 4)),
            pltpu.SemaphoreType.DMA((2,)),
            pltpu.SemaphoreType.DMA((2,)),
            pltpu.SemaphoreType.DMA((ny,)),
            pltpu.SemaphoreType.DMA((ny,)),
            pltpu.SemaphoreType.DMA((2,)),
        ],
        compiler_params=pltpu.CompilerParams(
            collective_id=0, has_side_effects=True, vmem_limit_bytes=36 * 1024 * 1024),
    )(*[pltpu.with_memory_space_constraint(array, pltpu.HBM)
        for array in (neighbors.T, embeddings, quality.reshape(blk, 128), probes)])
    first = total1.astype(F32) * quality[None, :] - probes
    second = 2.0 * (total2.astype(F32) * quality[None, :] - first) - probes
    return first, second


def solution(mesh):
    placed = (P("row", "col"), P("row"), P(None, "row"), P("row", None))
    return jax.shard_map(
        body,
        mesh=mesh,
        in_specs=placed,
        out_specs=(P(None, "row"), P(None, "row")),
        check_vma=False,
    )
```
